32 devices in a mesh: frame: 4 (over y, x), head: 8 (over z, core).
Axes of the slice: x: 2, y: 2, z: 4, core: 2. Of those that a mesh axis runs over, the one named last changes fastest.
Arguments:
- tokens: bfloat16 [4096, 5120], P('frame', 'head'), may hold values from -16 to 16
- qkv_weight: bfloat16 [3, 5120, 2048], P(None, None, 'head'), may hold values from -0.1118034 to 0.1118034
- out_weight: bfloat16 [2048, 5120], P('head'), may hold values from -0.1875 to 0.1875
- modulation: float32 [3, 5120], replicated, may hold values from -3 to 3
- block_mask: int32 [16, 32, 32], P('head', 'frame'), may hold values from 0 to 1, as said below
Outputs:
- mixed: bfloat16 [4096, 5120], P('frame', 'head')
The draws below stay inside these ranges and needn't reach their ends.
Inputs may be any that keep to these rules, and one draw needn't show every extreme that they name: `block_mask`: 1 keeps a pair of 128-token blocks; every query block keeps its own block.
All inputs are finite; a program needn't handle non-finite values.
Results may differ from the reference program's by a relative error of at most 0.0085.
Values may be sent and summed in bfloat16 or wider, within the bound.
A program may use at most 256 MiB of HBM per device.

```python
import math
import jax
import jax.numpy as jnp
from jax import lax

D = 5120
HD = 128
BLK = 128
TPF = 1024
HEADS = 16
N_FRAME = 4


def draw_tokens(key, part):
    first, second = jax.random.split(key, 2)
    seq_len = TPF * N_FRAME
    place = jnp.arange(D, dtype=jnp.float32) / (D - 1)
    rough = jax.random.uniform(second, (D,), jnp.float32, 0.5, 1.5)
    column = 1.0 + 2.0 * place
    values = jax.random.normal(first, (seq_len, D), jnp.float32) * column * rough
    return jnp.clip(values, -16.0, 16.0).astype(jnp.bfloat16)


def draw_qkv_weight(key, part):
    first = jax.random.fold_in(key, 0)
    width = HEADS * HD
    limit = 8.0 / math.sqrt(D)
    values = jax.random.normal(first, (3, D, width), jnp.float32) / math.sqrt(D)
    return jnp.clip(values, -limit, limit).astype(jnp.bfloat16)


def draw_modulation(key, part):
    first, second, third, fourth = jax.random.split(key, 4)
    rough = jax.random.uniform(fourth, (D,), jnp.float32, 0.5, 1.5)
    shift = jnp.clip(0.5 * jax.random.normal(first, (D,), jnp.float32) * rough, -2.5, 2.5)
    scale = jax.random.uniform(second, (D,), jnp.float32, -0.2, 1.0)
    gate = jax.random.uniform(third, (D,), jnp.float32, 0.5, 1.5)
    return jnp.stack([shift, scale, gate])


def draw_block_mask(key, part):
    first, second, third = jax.random.split(key, 3)
    per_frame = TPF // BLK
    frame_count = N_FRAME
    blocks = TPF * N_FRAME // BLK
    spatial = jax.random.randint(first, (HEADS, 1, 1), 0, 2)
    chosen = jax.random.randint(second, (HEADS, frame_count, frame_count), 0, 4) == 0
    extra = jax.random.randint(third, (HEADS, blocks, blocks), 0, 2) == 1
    query_block = jnp.arange(blocks, dtype=jnp.int32)[:, None]
    key_block = jnp.arange(blocks, dtype=jnp.int32)[None, :]
    query_frame = query_block // per_frame
    key_frame = key_block // per_frame
    same = query_frame == key_frame
    pair_chosen = jnp.take_along_axis(chosen.reshape(HEADS, frame_count * frame_count), (query_frame * frame_count + key_frame).reshape(1, -1) * jnp.ones((HEADS, 1), jnp.int32), axis=1).reshape(HEADS, blocks, blocks)
    spatial_keep = same[None] | pair_chosen & extra
    temporal_keep = (key_block % per_frame == query_block % per_frame)[None] | (same & (jnp.abs(query_block - key_block) <= 1))[None]
    keep = jnp.where(spatial == 1, spatial_keep, temporal_keep)
    return keep.astype(jnp.int32)


def spiked(drawn, own_key, source, target, parts, factor):
    owner, partner = [(jnp.arange(drawn.shape[dim]) // (drawn.shape[dim] // parts)).reshape([-1 if axis == dim else 1 for axis in range(drawn.ndim)]) for dim in (source, target)]
    chosen = jax.random.permutation(own_key, parts)[partner]
    strong = (owner == chosen) | (owner == (partner + parts // 2) % parts)
    return jnp.where(strong, factor * drawn, drawn)


def level_of(rng, shape, shards, low, high):
    level, own = 1.0, jax.random.fold_in(rng, 6)
    for dim, shards_of in shards:
        steps = jnp.exp(jax.random.uniform(jax.random.fold_in(own, dim), (shards_of,), jnp.float32, low / len(shards), high / len(shards)))
        level = level * jnp.repeat(steps, shape[dim] // shards_of).reshape([-1 if axis == dim else 1 for axis in range(len(shape))])
    return level


def bell_draw_with(key, extent, scale, reach, pieces, heavy, held_as=jnp.bfloat16):
    values = scale * jax.random.normal(key, extent, jnp.float32)
    if pieces:
        values = values * level_of(key, extent, pieces, -0.22, 0.18)
    return jnp.clip(spiked(values, jax.random.fold_in(key, 3), *heavy), -reach, reach).astype(held_as)


def setup_inputs(seed: int = 0) -> dict:
    splits = jax.random.split(jax.random.key(seed), 6)
    return {
        "tokens": draw_tokens(jax.random.fold_in(splits[5], 71), 0),
        "qkv_weight": draw_qkv_weight(jax.random.fold_in(splits[5], 71), 0),
        "out_weight": bell_draw_with(splits[2], (HEADS * HD, D), (HEADS * HD) ** -0.5, 0.1875, ((0, 8),), (0, 1, 8, 2.0)),
        "modulation": draw_modulation(jax.random.fold_in(splits[5], 71), 0),
        "block_mask": draw_block_mask(jax.random.fold_in(splits[5], 71), 0),
    }


def reference(tokens, qkv_weight, out_weight, modulation, block_mask):
    wide = tokens.astype(jnp.float32)
    center = lax.optimization_barrier(jnp.mean(wide, axis=1, keepdims=True))
    spread = lax.optimization_barrier(jnp.mean(jnp.square(wide - center), axis=1, keepdims=True))
    normed = ((wide - center) * lax.rsqrt(spread + 1e-06) * (1.0 + modulation[1]) + modulation[0]).astype(jnp.bfloat16)
    query = jnp.dot(normed, qkv_weight[0], preferred_element_type=jnp.float32).astype(jnp.bfloat16)
    keyed = jnp.dot(normed, qkv_weight[1], preferred_element_type=jnp.float32).astype(jnp.bfloat16)
    valued = jnp.dot(normed, qkv_weight[2], preferred_element_type=jnp.float32).astype(jnp.bfloat16)
    seq_len = tokens.shape[0]
    heads_count = block_mask.shape[0]
    head_size = qkv_weight.shape[2] // heads_count
    scale = 1.0 / math.sqrt(head_size)

    def split_heads(values):
        return values.reshape(seq_len, heads_count, head_size).transpose(1, 0, 2)

    def one_head(items):
        head_query, head_key, head_value, head_mask = items
        keep = jnp.repeat(jnp.repeat(head_mask > 0, BLK, axis=0), BLK, axis=1)
        scores = jnp.dot(head_query, head_key.T, preferred_element_type=jnp.float32) * scale
        masked = jnp.where(keep, scores, -jnp.inf)
        top = lax.optimization_barrier(jnp.max(masked, axis=1, keepdims=True))
        weights = jnp.where(keep, jnp.exp(scores - top), 0.0)
        total = lax.optimization_barrier(jnp.sum(weights, axis=1, keepdims=True))
        summed = jnp.dot(weights.astype(jnp.bfloat16), head_value, preferred_element_type=jnp.float32)
        return (summed / total).astype(jnp.bfloat16)
    heads_done = lax.map(one_head, (split_heads(query), split_heads(keyed), split_heads(valued), block_mask))
    heads_out = heads_done.transpose(1, 0, 2).reshape(seq_len, heads_count * head_size)
    projected = jnp.dot(heads_out, out_weight, preferred_element_type=jnp.float32)
    return (wide + modulation[2] * projected).astype(jnp.bfloat16)
```

```python
import functools
import math

import jax
import jax.numpy as jnp
from jax import lax
from jax.experimental import pallas as pl
from jax.experimental.pallas import tpu as pltpu
from jax.sharding import PartitionSpec as P

BLK = 128
NEGATIVE = -1e30
EPSILON = 1e-06
LOG2E = math.log2(math.e)
CHUNKS = 8


def source_of(me, size, step):
    if size & (size - 1) == 0:
        return lax.bitwise_xor(me, step)
    return lax.rem(me + size - step, size)


def target_of(me, size, step):
    if size & (size - 1) == 0:
        return lax.bitwise_xor(me, step)
    return lax.rem(me + step, size)


def chain(me, size):
    return me // 2, me % 2, me + 1 - 2 * (me % 2)


def send(src, dst, send_sem, recv_sem, **where):
    return pltpu.make_async_remote_copy(
        src_ref=src,
        dst_ref=dst,
        send_sem=send_sem,
        recv_sem=recv_sem,
        device_id=where,
        device_id_type=pl.DeviceIdType.MESH,
    )


class Relay:
    def __init__(self, me, size, buffer, span, sems):
        self.me, self.size, self.buffer, self.span = me, size, buffer, span
        self.spot, self.core, self.other = chain(me, size)
        self.line = size // 2
        self.far_send, self.far_recv, self.pair_send, self.pair_recv = sems

    def rows(self, block, chunk):
        start = pl.multiple_of(chunk * self.span, self.span)
        return self.buffer.at[block, pl.ds(start, self.span), :]

    def hop(self, block, chunk, away, source=None):
        ref = self.rows(block, chunk)
        slot = 0 if away > 0 else 1
        return send(
            ref if source is None else source,
            ref,
            self.far_send.at[block // 2, chunk, slot],
            self.far_recv.at[block // 2, chunk],
            head=self.me + 2 * away,
        )

    def pair(self, block, chunk, source=None):
        ref = self.rows(block, chunk)
        return send(
            ref if source is None else source,
            ref,
            self.pair_send.at[block // 2, chunk],
            self.pair_recv.at[block // 2, chunk],
            head=self.other,
        )

    def own(self, chunk, source=None):
        for away in (1, -1):
            edge = self.spot < self.line - 1 if away > 0 else self.spot > 0

            @pl.when(edge)
            def _():
                self.hop(self.me, chunk, away, source).start()

        self.pair(self.me, chunk, source).start()

    def pass_on(self, chunk, distance, ends=None):
        for away in (1, -1):
            spot = self.spot - away * distance
            here = spot >= 0 if away > 0 else spot < self.line
            edge = self.spot < self.line - 1 if away > 0 else self.spot > 0
            block = spot * 2 + self.core
            if ends is not None:
                far = 0 if away > 0 else self.line - 1
                here = spot == far if ends else jnp.logical_and(here, spot != far)

            @pl.when(here)
            def _():
                self.hop(block, chunk, away).wait_recv()

                @pl.when(edge)
                def _():
                    self.hop(block, chunk, away).start()

                self.pair(block, chunk).start()

    def advance(self, turn, count):
        for distance in range(1, self.line):
            chunk = turn - (distance - 1)

            @pl.when(jnp.logical_and(chunk >= 0, chunk < count))
            def _():
                self.pass_on(chunk, distance)

    def pass_all(self, chunk, ends):
        for distance in range(1, self.line):
            self.pass_on(chunk, distance, ends)

    def collect(self, chunk):
        for spot in range(self.line):
            self.pair(spot * 2 + 1 - self.core, chunk).wait_recv()

    def drain(self, chunk):
        for spot in range(self.line):
            block = spot * 2 + self.core
            self.pair(block, chunk).wait_send()
            for away in (1, -1):
                came = spot <= self.spot if away > 0 else spot >= self.spot
                edge = self.spot < self.line - 1 if away > 0 else self.spot > 0

                @pl.when(jnp.logical_and(came, edge))
                def _():
                    self.hop(block, chunk, away).wait_send()


def greet(me, frame, heads_axis, frames):
    barrier = pltpu.get_barrier_semaphore()
    for s in range(1, frames):
        pl.semaphore_signal(
            barrier, inc=1, device_id={"frame": target_of(frame, frames, s)},
            device_id_type=pl.DeviceIdType.MESH,
        )
    for s in range(1, heads_axis):
        pl.semaphore_signal(
            barrier, inc=1, device_id={"head": target_of(me, heads_axis, s)},
            device_id_type=pl.DeviceIdType.MESH,
        )
    pl.semaphore_wait(barrier, frames + heads_axis - 2)


def contract(parts, weight):
    cols = parts[0].shape[1]
    if cols % 128 == 0:
        return jnp.dot(
            jnp.concatenate(parts, axis=1), weight, preferred_element_type=jnp.float32
        )
    total = 0.0
    for i, part in enumerate(parts):
        total += jnp.dot(
            part, weight[i * cols : (i + 1) * cols], preferred_element_type=jnp.float32
        )
    return total


def block_kernel(
    frames, heads_axis, heads, count, w_slice, tokens, modulation, weight, out_weight, mask_ref,
    gate, out_ref, got, held, q_ref, kv_ref, band_ref, full, done,
    t_far_send, t_far_recv, t_pair_send, t_pair_recv,
    h_far_send, h_far_recv, h_pair_send, h_pair_recv,
    kv_send, kv_recv, w_send, w_recv, x_send, x_recv, local,
):
    me, frame = lax.axis_index("head"), lax.axis_index("frame")
    rows, cols = tokens.shape
    span = rows // count
    inner = q_ref.shape[1]
    width = cols * heads_axis
    line = heads_axis // 2
    share = band_ref.shape[1]
    head_size = inner // heads
    factor = LOG2E / math.sqrt(head_size)
    wide = span // BLK
    inside = jnp.logical_and(me // 2 > 0, me // 2 < line - 1)

    load = pltpu.make_async_copy(weight, held, local.at[0])
    load.start()
    mine = pltpu.make_async_copy(tokens, got.at[me], local.at[1])
    mine.start()
    band = pl.ds(pl.multiple_of(frame * share, share), share)
    keep = pltpu.make_async_copy(w_slice(out_weight, band, me), band_ref.at[me], local.at[2])
    keep.start()
    greet(me, frame, heads_axis, frames)
    relay = Relay(me, heads_axis, got, span, (t_far_send, t_far_recv, t_pair_send, t_pair_recv))
    spread = Relay(me, heads_axis, done, span, (h_far_send, h_far_recv, h_pair_send, h_pair_recv))

    def rows_of(chunk):
        return pl.ds(pl.multiple_of(chunk * span, span), span)

    def begin(chunk, carry):
        relay.own(chunk, tokens.at[rows_of(chunk), :])
        return carry

    lax.fori_loop(0, count, begin, 0)
    mine.wait()
    load.wait()

    def to_frame(chunk, s):
        window = rows_of(chunk)
        return send(
            kv_ref.at[0, :, window, :],
            kv_ref.at[s, :, window, :],
            kv_send.at[chunk, s],
            kv_recv.at[chunk, s],
            frame=target_of(frame, frames, s),
        )

    def to_head(s):
        there = target_of(me, heads_axis, s)
        return send(
            w_slice(out_weight, band, there), band_ref.at[me], w_send.at[s], w_recv.at[s],
            head=there,
        )

    def band_to(s):
        return send(
            band_ref, full.at[:, band, :], x_send.at[s], x_recv.at[s],
            frame=target_of(frame, frames, s),
        )

    def band_from(s):
        there = source_of(frame, frames, s)
        part = pl.ds(pl.multiple_of(there * share, share), share)
        return send(
            full.at[:, part, :], full.at[:, part, :], x_send.at[s], x_recv.at[s],
            frame=target_of(frame, frames, s),
        )

    late = max(line - 2, 0)

    def turn(i, carry):
        relay.advance(i, count)

        @pl.when(i == count + late - 2)
        def _():
            for s in range(1, heads_axis):
                to_head(s).start()

        @pl.when(i >= late)
        def _():
            step(i - late)

        return carry

    def step(chunk):
        relay.collect(chunk)
        window = rows_of(chunk)
        total = jnp.zeros((span, cols), jnp.float32)
        for i in range(heads_axis):
            total += got[i, window, :].astype(jnp.float32)
        center = jnp.sum(total, axis=1, keepdims=True) / width
        square = jnp.zeros((span, cols), jnp.float32)
        for i in range(heads_axis):
            off = got[i, window, :].astype(jnp.float32) - center
            square += off * off
        inverse = lax.rsqrt(jnp.sum(square, axis=1, keepdims=True) / width + EPSILON)
        parts = []
        for i in range(heads_axis):
            wide_part = got[i, window, :].astype(jnp.float32)
            shift = modulation[0:1, i * cols : (i + 1) * cols]
            gain = modulation[1:2, i * cols : (i + 1) * cols]
            parts.append(
                ((wide_part - center) * inverse * (1.0 + gain) + shift).astype(jnp.bfloat16)
            )
        sums = [contract(parts, held[j]) for j in range(3)]
        q_ref[window, :] = sums[0].astype(q_ref.dtype)
        kv_ref[0, 0, window, :] = sums[1].astype(kv_ref.dtype)
        kv_ref[0, 1, window, :] = sums[2].astype(kv_ref.dtype)
        for s in range(1, frames):
            to_frame(chunk, s).start()

    lax.fori_loop(0, count + late, turn, 0)

    def arrive(chunk, carry):
        for s in range(1, frames):
            to_frame(chunk, s).wait_recv()
        return carry

    lax.fori_loop(0, count, arrive, 0)
    sources = [source_of(frame, frames, s) * (rows // BLK) for s in range(frames)]

    def tile(t, carry):
        window = rows_of(t)
        for h in range(heads):
            lanes = slice(h * head_size, (h + 1) * head_size)
            query = q_ref[window, lanes]
            top = jnp.full((1, span), NEGATIVE, jnp.float32)
            total = jnp.zeros((1, span), jnp.float32)
            summed = jnp.zeros((head_size, span), jnp.float32)
            for slot in range(frames):
                scores = lax.dot_general(
                    kv_ref[slot, 0, :, lanes], query, (((1,), (1,)), ((), ())),
                    preferred_element_type=jnp.float32,
                )
                pieces = []
                new_top = top
                for block in range(rows // BLK):
                    row = jnp.concatenate(
                        [
                            jnp.full(
                                (1, BLK),
                                jnp.where(
                                    mask_ref[h, t * wide + k, sources[slot] + block] > 0,
                                    0.0,
                                    NEGATIVE,
                                ),
                                jnp.float32,
                            )
                            for k in range(wide)
                        ],
                        axis=1,
                    )
                    part = scores[block * BLK : (block + 1) * BLK] * factor + row
                    new_top = jnp.maximum(new_top, jnp.max(part, axis=0, keepdims=True))
                    pieces.append(part)
                fade = jnp.exp2(top - new_top)
                total = total * fade
                weights = [jnp.exp2(p - new_top) for p in pieces]
                for w in weights:
                    total += jnp.sum(w, axis=0, keepdims=True)
                joined = jnp.concatenate([w.astype(jnp.bfloat16) for w in weights], axis=0)
                summed = summed * fade + lax.dot_general(
                    kv_ref[slot, 1, :, lanes], joined, (((0,), (0,)), ((), ())),
                    preferred_element_type=jnp.float32,
                )
                top = new_top
            done[me, window, lanes] = (summed / total).T.astype(done.dtype)

        spread.own(t)

        @pl.when(jnp.logical_and(inside, t >= 1))
        def _():
            spread.pass_all(t - 1, False)

        return carry

    lax.fori_loop(0, count, tile, 0)

    keep.wait()
    for s in range(1, heads_axis):
        there = source_of(me, heads_axis, s)
        ref = band_ref.at[there]
        send(ref, ref, w_send.at[s], w_recv.at[s], head=target_of(me, heads_axis, s)).wait_recv()
    lay = pltpu.make_async_copy(band_ref, full.at[:, band, :], local.at[3])
    lay.start()
    for s in range(1, frames):
        band_to(s).start()

    def near(t, carry):
        spread.pass_all(t, False)
        return carry

    lax.fori_loop(jnp.where(inside, count - 1, 0), count, near, 0)
    lay.wait()

    def out(t):
        spread.collect(t)
        window = rows_of(t)
        plane = full[...].reshape(heads_axis * inner, full.shape[2])
        total = contract([done[i, window, :] for i in range(heads_axis)], plane)
        if gate.shape[1] == out_ref.shape[1]:
            own = gate[...]
        else:
            own = gate[2:3, pl.ds(pl.multiple_of(me * cols, cols), cols)]
        wide_part = got[me, window, :].astype(jnp.float32)
        out_ref[window, :] = (wide_part + own * total).astype(out_ref.dtype)

    def last(t, carry):
        @pl.when(t < count)
        def _():
            spread.pass_all(t, True)

        @pl.when(t == 0)
        def _():
            for s in range(1, frames):
                band_from(s).wait_recv()

        @pl.when(t >= 1)
        def _():
            out(t - 1)

        return carry

    lax.fori_loop(0, count + 1, last, 0)

    def finish(chunk, carry):
        relay.drain(chunk)
        spread.drain(chunk)
        for s in range(1, frames):
            to_frame(chunk, s).wait_send()
        return carry

    lax.fori_loop(0, count, finish, 0)
    for s in range(1, heads_axis):
        to_head(s).wait_send()
    for s in range(1, frames):
        band_to(s).wait_send()


def sublayer(frames, heads_axis, heads, tokens, modulation, weight, out_weight, mask, gate):
    rows, cols = tokens.shape
    inner = weight.shape[2]
    count = CHUNKS
    line = heads_axis // 2
    whole = pl.BlockSpec(memory_space=pltpu.VMEM)
    away = pl.BlockSpec(memory_space=pl.ANY)
    sem = pltpu.SemaphoreType.DMA
    if cols % 128 == 0:
        def w_slice(ref, band, there):
            return ref.at[band, pl.ds(pl.multiple_of(there * cols, cols), cols)]
    else:
        out_weight = out_weight.reshape(inner, heads_axis, cols).transpose(1, 0, 2)

        def w_slice(ref, band, there):
            return ref.at[there, band, :]

    relay_sems = [sem((line, count, 2)), sem((line, count)), sem((line, count)), sem((line, count))]
    return pl.pallas_call(
        functools.partial(block_kernel, frames, heads_axis, heads, count, w_slice),
        in_specs=[
            away, whole, away, away, pl.BlockSpec(memory_space=pltpu.SMEM), whole,
        ],
        out_specs=whole,
        out_shape=jax.ShapeDtypeStruct((rows, cols), jnp.bfloat16),
        scratch_shapes=[
            pltpu.VMEM((heads_axis, rows, cols), jnp.bfloat16),
            pltpu.VMEM(weight.shape, jnp.bfloat16),
            pltpu.VMEM((rows, inner), jnp.bfloat16),
            pltpu.VMEM((frames, 2, rows, inner), jnp.bfloat16),
            pltpu.VMEM((heads_axis, inner // frames, cols), jnp.bfloat16),
            pltpu.VMEM((heads_axis, inner, cols), jnp.bfloat16),
            pltpu.VMEM((heads_axis, rows, inner), jnp.bfloat16),
            *relay_sems,
            *relay_sems,
            sem((count, frames)),
            sem((count, frames)),
            sem((heads_axis,)),
            sem((heads_axis,)),
            sem((frames,)),
            sem((frames,)),
            sem((4,)),
        ],
        compiler_params=pltpu.CompilerParams(collective_id=0, has_side_effects=True),
        name="sublayer",
    )(tokens, modulation, weight, out_weight, mask, gate)


def shards(frames, heads_axis, tokens, qkv_weight, out_weight, modulation, block_mask):
    local_cols = tokens.shape[1]
    gate = modulation
    if local_cols % 128:
        head = lax.axis_index("head")
        gate = lax.dynamic_slice_in_dim(modulation[2:3], head * local_cols, local_cols, 1)
    return sublayer(
        frames, heads_axis, block_mask.shape[0], tokens, modulation, qkv_weight, out_weight,
        block_mask, gate,
    )


def solution(mesh):
    placed = (
        P("frame", "head"),
        P(None, None, "head"),
        P("head", None),
        P(),
        P("head", "frame", None),
    )
    body = functools.partial(shards, mesh.shape["frame"], mesh.shape["head"])
    return jax.shard_map(
        body, mesh=mesh, in_specs=placed, out_specs=P("frame", "head"), check_vma=False
    )
```

```python
import functools
import math

import jax
import jax.numpy as jnp
from jax import lax
from jax.experimental import pallas as pl
from jax.experimental.pallas import tpu as pltpu
from jax.sharding import PartitionSpec as P

BLK = 128
NEGATIVE = -1e30
EPSILON = 1e-06
LOG2E = math.log2(math.e)
CHUNKS = 8
AHEAD = 2


def source_of(me, size, step):
    if size & (size - 1) == 0:
        return lax.bitwise_xor(me, step)
    return lax.rem(me + size - step, size)


def target_of(me, size, step):
    if size & (size - 1) == 0:
        return lax.bitwise_xor(me, step)
    return lax.rem(me + step, size)


def chain(me, size):
    return me // 2, me % 2, me + 1 - 2 * (me % 2)


def send(src, dst, send_sem, recv_sem, **where):
    return pltpu.make_async_remote_copy(
        src_ref=src,
        dst_ref=dst,
        send_sem=send_sem,
        recv_sem=recv_sem,
        device_id=where,
        device_id_type=pl.DeviceIdType.MESH,
    )


class Relay:
    def __init__(self, me, size, buffer, span, sems):
        self.me, self.size, self.buffer, self.span = me, size, buffer, span
        self.spot, self.core, self.other = chain(me, size)
        self.line = size // 2
        self.far_send, self.far_recv, self.pair_send, self.pair_recv = sems

    def rows(self, block, chunk):
        start = pl.multiple_of(chunk * self.span, self.span)
        return self.buffer.at[block, pl.ds(start, self.span), :]

    def hop(self, block, chunk, away, source=None):
        ref = self.rows(block, chunk)
        slot = 0 if away > 0 else 1
        return send(
            ref if source is None else source,
            ref,
            self.far_send.at[block // 2, chunk, slot],
            self.far_recv.at[block // 2, chunk],
            head=self.me + 2 * away,
        )

    def pair(self, block, chunk, source=None):
        ref = self.rows(block, chunk)
        return send(
            ref if source is None else source,
            ref,
            self.pair_send.at[block // 2, chunk],
            self.pair_recv.at[block // 2, chunk],
            head=self.other,
        )

    def own(self, chunk, source=None):
        for away in (1, -1):
            edge = self.spot < self.line - 1 if away > 0 else self.spot > 0

            @pl.when(edge)
            def _():
                self.hop(self.me, chunk, away, source).start()

        self.pair(self.me, chunk, source).start()

    def pass_on(self, chunk, distance, ends=None):
        for away in (1, -1):
            spot = self.spot - away * distance
            here = spot >= 0 if away > 0 else spot < self.line
            edge = self.spot < self.line - 1 if away > 0 else self.spot > 0
            block = spot * 2 + self.core
            if ends is not None:
                far = 0 if away > 0 else self.line - 1
                here = spot == far if ends else jnp.logical_and(here, spot != far)

            @pl.when(here)
            def _():
                self.hop(block, chunk, away).wait_recv()

                @pl.when(edge)
                def _():
                    self.hop(block, chunk, away).start()

                self.pair(block, chunk).start()

    def advance(self, turn, count, ends=None):
        for distance in range(1, self.line):
            chunk = turn - (distance - 1)

            @pl.when(jnp.logical_and(chunk >= 0, chunk < count))
            def _():
                self.pass_on(chunk, distance, ends)

    def pass_all(self, chunk, ends):
        for distance in range(1, self.line):
            self.pass_on(chunk, distance, ends)

    def collect(self, chunk):
        for spot in range(self.line):
            self.pair(spot * 2 + 1 - self.core, chunk).wait_recv()

    def drain(self, chunk):
        for spot in range(self.line):
            block = spot * 2 + self.core
            self.pair(block, chunk).wait_send()
            for away in (1, -1):
                came = spot <= self.spot if away > 0 else spot >= self.spot
                edge = self.spot < self.line - 1 if away > 0 else self.spot > 0

                @pl.when(jnp.logical_and(came, edge))
                def _():
                    self.hop(block, chunk, away).wait_send()


def greet(me, frame, heads_axis, frames):
    barrier = pltpu.get_barrier_semaphore()
    for s in range(1, frames):
        pl.semaphore_signal(
            barrier, inc=1, device_id={"frame": target_of(frame, frames, s)},
            device_id_type=pl.DeviceIdType.MESH,
        )
    for s in range(1, heads_axis):
        pl.semaphore_signal(
            barrier, inc=1, device_id={"head": target_of(me, heads_axis, s)},
            device_id_type=pl.DeviceIdType.MESH,
        )
    pl.semaphore_wait(barrier, frames + heads_axis - 2)


def contract(parts, weight):
    cols = parts[0].shape[1]
    if cols % 128 == 0:
        return jnp.dot(
            jnp.concatenate(parts, axis=1), weight, preferred_element_type=jnp.float32
        )
    total = 0.0
    for i, part in enumerate(parts):
        total += jnp.dot(
            part, weight[i * cols : (i + 1) * cols], preferred_element_type=jnp.float32
        )
    return total


def block_kernel(
    frames, heads_axis, heads, count, w_slice, tokens, modulation, weight, out_weight, mask_ref,
    gate, out_ref, got, held, q_ref, kv_ref, band_ref, full, done,
    t_far_send, t_far_recv, t_pair_send, t_pair_recv,
    h_far_send, h_far_recv, h_pair_send, h_pair_recv,
    kv_send, kv_recv, w_send, w_recv, x_send, x_recv, local,
):
    me, frame = lax.axis_index("head"), lax.axis_index("frame")
    rows, cols = tokens.shape
    span = rows // count
    inner = q_ref.shape[1]
    width = cols * heads_axis
    line = heads_axis // 2
    share = band_ref.shape[1]
    head_size = inner // heads
    factor = LOG2E / math.sqrt(head_size)
    wide = span // BLK
    inside = jnp.logical_and(me // 2 > 0, me // 2 < line - 1)

    load = pltpu.make_async_copy(weight, held, local.at[0])
    load.start()
    mine = pltpu.make_async_copy(tokens, got.at[me], local.at[1])
    mine.start()
    band = pl.ds(pl.multiple_of(frame * share, share), share)
    keep = pltpu.make_async_copy(w_slice(out_weight, band, me), band_ref.at[me], local.at[2])
    keep.start()
    greet(me, frame, heads_axis, frames)
    relay = Relay(me, heads_axis, got, span, (t_far_send, t_far_recv, t_pair_send, t_pair_recv))
    spread = Relay(me, heads_axis, done, span, (h_far_send, h_far_recv, h_pair_send, h_pair_recv))

    def rows_of(chunk):
        return pl.ds(pl.multiple_of(chunk * span, span), span)

    def begin(chunk, carry):
        relay.own(chunk, tokens.at[rows_of(chunk), :])
        return carry

    def to_frame(chunk, s):
        window = rows_of(chunk)
        return send(
            kv_ref.at[0, :, window, :],
            kv_ref.at[s, :, window, :],
            kv_send.at[chunk, s],
            kv_recv.at[chunk, s],
            frame=target_of(frame, frames, s),
        )

    def to_head(s):
        there = target_of(me, heads_axis, s)
        return send(
            w_slice(out_weight, band, there), band_ref.at[me], w_send.at[s], w_recv.at[s],
            head=there,
        )

    def band_in(s):
        ref = band_ref.at[source_of(me, heads_axis, s)]
        return send(
            ref, ref, w_send.at[s], w_recv.at[s], head=target_of(me, heads_axis, s)
        )

    lay = pltpu.make_async_copy(band_ref, full.at[:, band, :], local.at[3])

    def band_to(s):
        return send(
            band_ref, full.at[:, band, :], x_send.at[s], x_recv.at[s],
            frame=target_of(frame, frames, s),
        )

    def band_from(s):
        there = source_of(frame, frames, s)
        part = pl.ds(pl.multiple_of(there * share, share), share)
        return send(
            full.at[:, part, :], full.at[:, part, :], x_send.at[s], x_recv.at[s],
            frame=target_of(frame, frames, s),
        )

    late = max(line - 2, 0)
    for s in range(1, heads_axis):
        to_head(s).start()
    lax.fori_loop(0, AHEAD, begin, 0)
    mine.wait()
    load.wait()

    def turn(i, carry):
        @pl.when(i + AHEAD < count)
        def _():
            begin(i + AHEAD, 0)

        @pl.when(i == 1)
        def _():
            keep.wait()
            for s in range(1, heads_axis):
                band_in(s).wait_recv()
            lay.start()
            for s in range(1, frames):
                band_to(s).start()

        relay.advance(i, count)

        @pl.when(i >= late)
        def _():
            step(i - late)

        return carry

    def step(chunk):
        relay.collect(chunk)
        window = rows_of(chunk)
        total = jnp.zeros((span, cols), jnp.float32)
        for i in range(heads_axis):
            total += got[i, window, :].astype(jnp.float32)
        center = jnp.sum(total, axis=1, keepdims=True) / width
        square = jnp.zeros((span, cols), jnp.float32)
        for i in range(heads_axis):
            off = got[i, window, :].astype(jnp.float32) - center
            square += off * off
        inverse = lax.rsqrt(jnp.sum(square, axis=1, keepdims=True) / width + EPSILON)
        parts = []
        for i in range(heads_axis):
            wide_part = got[i, window, :].astype(jnp.float32)
            shift = modulation[0:1, i * cols : (i + 1) * cols]
            gain = modulation[1:2, i * cols : (i + 1) * cols]
            parts.append(
                ((wide_part - center) * inverse * (1.0 + gain) + shift).astype(jnp.bfloat16)
            )
        sums = [contract(parts, held[j]) for j in range(3)]
        q_ref[window, :] = sums[0].astype(q_ref.dtype)
        kv_ref[0, 0, window, :] = sums[1].astype(kv_ref.dtype)
        kv_ref[0, 1, window, :] = sums[2].astype(kv_ref.dtype)
        for s in range(1, frames):
            to_frame(chunk, s).start()

    lax.fori_loop(0, count + late, turn, 0)

    def arrive(chunk, carry):
        for s in range(1, frames):
            to_frame(chunk, s).wait_recv()
        return carry

    lax.fori_loop(0, count, arrive, 0)
    sources = [source_of(frame, frames, s) * (rows // BLK) for s in range(frames)]

    def tile(t, carry):
        window = rows_of(t)
        for h in range(heads):
            lanes = slice(h * head_size, (h + 1) * head_size)
            query = q_ref[window, lanes]
            top = jnp.full((1, span), NEGATIVE, jnp.float32)
            total = jnp.zeros((1, span), jnp.float32)
            summed = jnp.zeros((head_size, span), jnp.float32)
            for slot in range(frames):
                scores = lax.dot_general(
                    kv_ref[slot, 0, :, lanes], query, (((1,), (1,)), ((), ())),
                    preferred_element_type=jnp.float32,
                )
                pieces = []
                new_top = top
                for block in range(rows // BLK):
                    row = jnp.concatenate(
                        [
                            jnp.full(
                                (1, BLK),
                                jnp.where(
                                    mask_ref[h, t * wide + k, sources[slot] + block] > 0,
                                    0.0,
                                    NEGATIVE,
                                ),
                                jnp.float32,
                            )
                            for k in range(wide)
                        ],
                        axis=1,
                    )
                    part = scores[block * BLK : (block + 1) * BLK] * factor + row
                    new_top = jnp.maximum(new_top, jnp.max(part, axis=0, keepdims=True))
                    pieces.append(part)
                fade = jnp.exp2(top - new_top)
                total = total * fade
                weights = [jnp.exp2(p - new_top) for p in pieces]
                for w in weights:
                    total += jnp.sum(w, axis=0, keepdims=True)
                joined = jnp.concatenate([w.astype(jnp.bfloat16) for w in weights], axis=0)
                summed = summed * fade + lax.dot_general(
                    kv_ref[slot, 1, :, lanes], joined, (((0,), (0,)), ((), ())),
                    preferred_element_type=jnp.float32,
                )
                top = new_top
            done[me, window, lanes] = (summed / total).T.astype(done.dtype)

        spread.own(t)

        @pl.when(jnp.logical_and(inside, t >= 1))
        def _():
            spread.pass_all(t - 1, False)

        return carry

    lax.fori_loop(0, count, tile, 0)

    def near(t, carry):
        spread.pass_all(t, False)
        return carry

    lax.fori_loop(jnp.where(inside, count - 1, 0), count, near, 0)
    lay.wait()

    def out(t):
        spread.collect(t)
        window = rows_of(t)
        plane = full[...].reshape(heads_axis * inner, full.shape[2])
        total = contract([done[i, window, :] for i in range(heads_axis)], plane)
        if gate.shape[1] == out_ref.shape[1]:
            own = gate[...]
        else:
            own = gate[2:3, pl.ds(pl.multiple_of(me * cols, cols), cols)]
        wide_part = got[me, window, :].astype(jnp.float32)
        out_ref[window, :] = (wide_part + own * total).astype(out_ref.dtype)

    for s in range(1, frames):
        band_from(s).wait_recv()

    behind = line - 1

    def last(i, carry):
        spread.advance(i, count, True)

        @pl.when(i >= behind)
        def _():
            out(i - behind)

        return carry

    lax.fori_loop(0, count + behind, last, 0)

    def finish(chunk, carry):
        relay.drain(chunk)
        spread.drain(chunk)
        for s in range(1, frames):
            to_frame(chunk, s).wait_send()
        return carry

    lax.fori_loop(0, count, finish, 0)
    for s in range(1, heads_axis):
        to_head(s).wait_send()
    for s in range(1, frames):
        band_to(s).wait_send()


def sublayer(frames, heads_axis, heads, tokens, modulation, weight, out_weight, mask, gate):
    rows, cols = tokens.shape
    inner = weight.shape[2]
    count = CHUNKS
    line = heads_axis // 2
    whole = pl.BlockSpec(memory_space=pltpu.VMEM)
    away = pl.BlockSpec(memory_space=pl.ANY)
    sem = pltpu.SemaphoreType.DMA
    if cols % 128 == 0:
        def w_slice(ref, band, there):
            return ref.at[band, pl.ds(pl.multiple_of(there * cols, cols), cols)]
    else:
        out_weight = out_weight.reshape(inner, heads_axis, cols).transpose(1, 0, 2)

        def w_slice(ref, band, there):
            return ref.at[there, band, :]

    relay_sems = [sem((line, count, 2)), sem((line, count)), sem((line, count)), sem((line, count))]
    return pl.pallas_call(
        functools.partial(block_kernel, frames, heads_axis, heads, count, w_slice),
        in_specs=[
            away, whole, away, away, pl.BlockSpec(memory_space=pltpu.SMEM), whole,
        ],
        out_specs=whole,
        out_shape=jax.ShapeDtypeStruct((rows, cols), jnp.bfloat16),
        scratch_shapes=[
            pltpu.VMEM((heads_axis, rows, cols), jnp.bfloat16),
            pltpu.VMEM(weight.shape, jnp.bfloat16),
            pltpu.VMEM((rows, inner), jnp.bfloat16),
            pltpu.VMEM((frames, 2, rows, inner), jnp.bfloat16),
            pltpu.VMEM((heads_axis, inner // frames, cols), jnp.bfloat16),
            pltpu.VMEM((heads_axis, inner, cols), jnp.bfloat16),
            pltpu.VMEM((heads_axis, rows, inner), jnp.bfloat16),
            *relay_sems,
            *relay_sems,
            sem((count, frames)),
            sem((count, frames)),
            sem((heads_axis,)),
            sem((heads_axis,)),
            sem((frames,)),
            sem((frames,)),
            sem((4,)),
        ],
        compiler_params=pltpu.CompilerParams(collective_id=0, has_side_effects=True),
        name="sublayer",
    )(tokens, modulation, weight, out_weight, mask, gate)


def shards(frames, heads_axis, tokens, qkv_weight, out_weight, modulation, block_mask):
    local_cols = tokens.shape[1]
    gate = modulation
    if local_cols % 128:
        head = lax.axis_index("head")
        gate = lax.dynamic_slice_in_dim(modulation[2:3], head * local_cols, local_cols, 1)
    return sublayer(
        frames, heads_axis, block_mask.shape[0], tokens, modulation, qkv_weight, out_weight,
        block_mask, gate,
    )


def solution(mesh):
    placed = (
        P("frame", "head"),
        P(None, None, "head"),
        P("head", None),
        P(),
        P("head", "frame", None),
    )
    body = functools.partial(shards, mesh.shape["frame"], mesh.shape["head"])
    return jax.shard_map(
        body, mesh=mesh, in_specs=placed, out_specs=P("frame", "head"), check_vma=False
    )
```

```python
import functools
import math

import jax
import jax.numpy as jnp
from jax import lax
from jax.experimental import pallas as pl
from jax.experimental.pallas import tpu as pltpu
from jax.sharding import PartitionSpec as P

BLK = 128
NEGATIVE = -1e30
EPSILON = 1e-06
LOG2E = math.log2(math.e)
AHEAD = 4
LAG = 2
GROUP = 4
VMEM_BYTES = 52 * 2**20


def source_of(me, size, step):
    if size & (size - 1) == 0:
        return lax.bitwise_xor(me, step)
    return lax.rem(me + size - step, size)


def target_of(me, size, step):
    if size & (size - 1) == 0:
        return lax.bitwise_xor(me, step)
    return lax.rem(me + step, size)


def chain(me, size):
    return me // 2, me % 2, me + 1 - 2 * (me % 2)


def send(src, dst, send_sem, recv_sem, **where):
    return pltpu.make_async_remote_copy(
        src_ref=src,
        dst_ref=dst,
        send_sem=send_sem,
        recv_sem=recv_sem,
        device_id=where,
        device_id_type=pl.DeviceIdType.MESH,
    )


class Relay:
    def __init__(self, me, size, buffer, span, sems):
        self.me, self.size, self.buffer, self.span = me, size, buffer, span
        self.spot, self.core, self.other = chain(me, size)
        self.line = size // 2
        self.far_send, self.far_recv, self.pair_send, self.pair_recv = sems

    def rows(self, block, chunk):
        start = pl.multiple_of(chunk * self.span, self.span)
        return self.buffer.at[block, pl.ds(start, self.span), :]

    def hop(self, block, chunk, away, source=None):
        ref = self.rows(block, chunk)
        return send(
            ref if source is None else source,
            ref,
            self.far_send.at[0],
            self.far_recv.at[block // 2, chunk],
            head=self.me + 2 * away,
        )

    def pair(self, block, chunk, source=None):
        ref = self.rows(block, chunk)
        return send(
            ref if source is None else source,
            ref,
            self.pair_send.at[0],
            self.pair_recv.at[chunk],
            head=self.other,
        )

    def own(self, chunk, source=None):
        for away in (1, -1):
            edge = self.spot < self.line - 1 if away > 0 else self.spot > 0

            @pl.when(edge)
            def _():
                self.hop(self.me, chunk, away, source).start()

        self.pair(self.me, chunk, source).start()

    def pass_on(self, chunk, distance, ends=None):
        for away in (1, -1):
            spot = self.spot - away * distance
            here = spot >= 0 if away > 0 else spot < self.line
            edge = self.spot < self.line - 1 if away > 0 else self.spot > 0
            block = spot * 2 + self.core
            if ends is not None:
                far = 0 if away > 0 else self.line - 1
                here = spot == far if ends else jnp.logical_and(here, spot != far)

            @pl.when(here)
            def _():
                self.hop(block, chunk, away).wait_recv()

                @pl.when(edge)
                def _():
                    self.hop(block, chunk, away).start()

                self.pair(block, chunk).start()

    def advance(self, turn, count, ends=None):
        for distance in range(1, self.line):
            chunk = turn - (distance - 1)

            @pl.when(jnp.logical_and(chunk >= 0, chunk < count))
            def _():
                self.pass_on(chunk, distance, ends)

    def pass_all(self, chunk, ends):
        for distance in range(1, self.line):
            self.pass_on(chunk, distance, ends)

    def collect(self, chunk):
        start = pl.multiple_of(chunk * self.span, self.span)
        ref = self.buffer.at[pl.ds(0, self.line), pl.ds(start, self.span), :]
        send(
            ref, ref, self.pair_send.at[0], self.pair_recv.at[chunk], head=self.other
        ).wait_recv()

    def sent(self, blocks, sem):
        ref = self.buffer.at[pl.ds(0, blocks)]
        send(ref, ref, sem, self.pair_recv.at[0], head=self.other).wait_send()

    def drain(self):
        self.sent(self.line, self.pair_send.at[0])
        for spot in range(self.line):
            up = spot + 1 if spot < self.line - 1 else 0
            down = self.line - spot if spot > 0 else 0
            if up + down:

                @pl.when(self.spot == spot)
                def _():
                    self.sent(up + down, self.far_send.at[0])


def greet(me, frame, heads_axis, frames):
    barrier = pltpu.get_barrier_semaphore()
    for s in range(1, frames):
        pl.semaphore_signal(
            barrier, inc=1, device_id={"frame": target_of(frame, frames, s)},
            device_id_type=pl.DeviceIdType.MESH,
        )
    for s in range(1, heads_axis):
        pl.semaphore_signal(
            barrier, inc=1, device_id={"head": target_of(me, heads_axis, s)},
            device_id_type=pl.DeviceIdType.MESH,
        )
    pl.semaphore_wait(barrier, frames + heads_axis - 2)


def contract(parts, weight):
    cols = parts[0].shape[1]
    if cols % 128 == 0:
        return jnp.dot(
            jnp.concatenate(parts, axis=1), weight, preferred_element_type=jnp.float32
        )
    total = 0.0
    for i, part in enumerate(parts):
        total += jnp.dot(
            part, weight[i * cols : (i + 1) * cols], preferred_element_type=jnp.float32
        )
    return total


def block_kernel(
    frames, heads_axis, heads, count, group, w_slice, tokens, adjust, weight, out_weight, mask_in,
    gate_in, out_ref, got, held, q_ref, kv_ref, band_ref, full, done,
    peak, mass, blend, mixed, modulation, gate, mask_ref,
    t_far_send, t_far_recv, t_pair_send, t_pair_recv,
    h_far_send, h_far_recv, h_pair_send, h_pair_recv,
    kv_send, kv_recv, w_send, w_recv, x_send, x_recv, local, o_sem,
):
    me, frame = lax.axis_index("head"), lax.axis_index("frame")
    rows, cols = tokens.shape
    span = rows // count
    inner = q_ref.shape[1]
    width = cols * heads_axis
    line = heads_axis // 2
    share = band_ref.shape[1]
    head_size = inner // heads
    factor = LOG2E / math.sqrt(head_size)
    inside = jnp.logical_and(me // 2 > 0, me // 2 < line - 1)

    load = pltpu.make_async_copy(weight, held, local.at[0])
    load.start()
    mine = pltpu.make_async_copy(tokens, got.at[me], local.at[1])
    mine.start()
    tune = pltpu.make_async_copy(adjust, modulation, local.at[4])
    tune.start()
    hide = pltpu.make_async_copy(mask_in, mask_ref, local.at[6])
    hide.start()
    open_gate = pltpu.make_async_copy(gate_in, gate, local.at[5])
    open_gate.start()
    band = pl.ds(pl.multiple_of(frame * share, share), share)
    keep = pltpu.make_async_copy(w_slice(out_weight, band, me), band_ref.at[me], local.at[2])
    keep.start()
    greet(me, frame, heads_axis, frames)
    relay = Relay(me, heads_axis, got, span, (t_far_send, t_far_recv, t_pair_send, t_pair_recv))
    spread = Relay(me, heads_axis, done, span, (h_far_send, h_far_recv, h_pair_send, h_pair_recv))

    def rows_of(chunk):
        return pl.ds(pl.multiple_of(chunk * span, span), span)

    def begin(chunk, carry):
        relay.own(chunk, tokens.at[rows_of(chunk), :])
        return carry

    square = frames == 4

    def to_frame(chunk, s):
        window = rows_of(chunk)
        return send(
            kv_ref.at[0, :, window, :],
            kv_ref.at[s, :, window, :],
            kv_send.at[0],
            kv_recv.at[chunk, s - 1],
            frame=target_of(frame, frames, s),
        )

    def over(chunk, half):
        window = rows_of(chunk)
        near, there = (1, 2) if half == 0 else (2, 1)
        return send(
            kv_ref.at[near, half, window, :],
            kv_ref.at[3, half, window, :],
            kv_send.at[0],
            kv_recv.at[chunk, 2],
            frame=target_of(frame, frames, there),
        )

    def far_pair(chunk):
        ref = kv_ref.at[3, :, rows_of(chunk), :]
        return send(
            ref, ref, kv_send.at[0], kv_recv.at[chunk, 2], frame=target_of(frame, frames, 1)
        )

    direct = (1, 2) if square else tuple(range(1, frames))

    def relay_pair(chunk):
        for half in range(2 if square else 0):
            to_frame(chunk, half + 1).wait_recv()
            over(chunk, half).start()

    def heard(chunk):
        if square:
            far_pair(chunk).wait_recv()
        else:
            for s in direct:
                to_frame(chunk, s).wait_recv()

    def to_head(s):
        there = target_of(me, heads_axis, s)
        return send(
            w_slice(out_weight, band, there), band_ref.at[me], w_send.at[0], w_recv.at[0],
            head=there,
        )

    def bands():
        ref = band_ref.at[pl.ds(0, heads_axis - 1)]
        return send(
            ref, ref, w_send.at[0], w_recv.at[0], head=target_of(me, heads_axis, 1)
        )

    lay = pltpu.make_async_copy(band_ref, full.at[:, band, :], local.at[3])

    part = heads_axis // 2

    def slot_of(s, p):
        return p if square and s == p + 1 else 2

    def band_to(s, p):
        some = pl.ds(p * part, part)
        return send(
            band_ref.at[some], full.at[some, band, :], x_send.at[0], x_recv.at[slot_of(s, p)],
            frame=target_of(frame, frames, s),
        )

    def band_over(p):
        near, there = (1, 2) if p == 0 else (2, 1)
        part_rows = pl.ds(pl.multiple_of(source_of(frame, frames, near) * share, share), share)
        ref = full.at[pl.ds(p * part, part), part_rows, :]
        return send(
            ref, ref, x_send.at[0], x_recv.at[2], frame=target_of(frame, frames, there)
        )

    def band_near(p):
        ref = full.at[pl.ds(p * part, part), pl.ds(0, share), :]
        return send(
            ref, ref, x_send.at[0], x_recv.at[p], frame=target_of(frame, frames, p + 1)
        )

    def band_rest(count_of, slot):
        ref = full.at[:, pl.ds(0, count_of * share), :]
        return send(
            ref, ref, x_send.at[0], x_recv.at[slot], frame=target_of(frame, frames, 1)
        )

    late = jnp.maximum(jnp.maximum(me // 2, line - 1 - me // 2) - 1, 0)

    def give(later):
        for s in range(1, heads_axis):
            spot = target_of(me, heads_axis, s) // 2
            edge = jnp.logical_or(spot == 0, spot == line - 1)
            wait = jnp.logical_and(edge, spot != me // 2)

            @pl.when(wait if later else jnp.logical_not(wait))
            def _():
                to_head(s).start()

    def share_out(turn):
        for s in direct:
            band_to(s, (turn + s + 1) % 2).start()

    def pass_band():
        for p in range(2 if square else 0):
            band_near(p).wait_recv()
            band_over(p).start()

    def take():
        keep.wait()
        bands().wait_recv()
        lay.start()
        share_out(0)

    give(False)
    lax.fori_loop(0, jnp.where(inside, AHEAD, count), begin, 0)
    mine.wait()
    load.wait()
    tune.wait()
    hide.wait()
    open_gate.wait()

    def step(chunk):
        relay.collect(chunk)
        window = rows_of(chunk)
        total = jnp.zeros((span, cols), jnp.float32)
        for i in range(heads_axis):
            total += got[i, window, :].astype(jnp.float32)
        center = jnp.sum(total, axis=1, keepdims=True) / width
        square = jnp.zeros((span, cols), jnp.float32)
        for i in range(heads_axis):
            off = got[i, window, :].astype(jnp.float32) - center
            square += off * off
        inverse = lax.rsqrt(jnp.sum(square, axis=1, keepdims=True) / width + EPSILON)
        parts = []
        for i in range(heads_axis):
            wide_part = got[i, window, :].astype(jnp.float32)
            shift = modulation[0:1, i * cols : (i + 1) * cols]
            gain = modulation[1:2, i * cols : (i + 1) * cols]
            parts.append(
                ((wide_part - center) * inverse * (1.0 + gain) + shift).astype(jnp.bfloat16)
            )
        sums = [contract(parts, held[j]) for j in range(3)]
        q_ref[window, :] = sums[0].astype(q_ref.dtype)
        kv_ref[0, 0, window, :] = sums[1].astype(kv_ref.dtype)
        kv_ref[0, 1, window, :] = sums[2].astype(kv_ref.dtype)
        for s in direct:
            to_frame(chunk, s).start()

    sources = [source_of(frame, frames, s) * count for s in range(frames)]

    groups = count // group

    def fold(c):
        early = count - 1 - LAG
        key = jnp.where(c < count - 1, c - LAG, early)

        @pl.when(jnp.logical_and(key >= 0, c != count - 1))
        def _():
            heard(key)

        def each(g, carry):
            ready = (g + 1) * group - 1

            def one(k, carry):
                @pl.when(c == count - 1)
                def _():
                    for at, chunk in ((1, count - 2), (4, count - 1)):

                        @pl.when(k == min(at, early - 1))
                        def _():
                            relay_pair(chunk)

                    @pl.when(jnp.logical_and(k == early - 1, jnp.logical_not(inside)))
                    def _():
                        take()
                        share_out(1)

                @pl.when(jnp.logical_and(c == count, jnp.logical_and(g == 0, k > key)))
                def _():
                    heard(k)

                weigh(g * group, k)

                @pl.when(k == count - 1)
                def _():
                    for a in range(group):
                        settle(g * group + a)

                    @pl.when(jnp.logical_and(inside, g > 0))
                    def _():
                        for a in range(group):
                            spread.pass_all((g - 1) * group + a, False)

                return carry

            first = jnp.where(
                c < count - 1, jnp.where(c == ready, 0, jnp.maximum(key, 0)),
                jnp.where(c == count - 1, 0, key),
            )
            last = jnp.where(
                c < count - 1, jnp.where(c >= ready, key + 1, 0),
                jnp.where(c == count - 1, jnp.where(g == groups - 1, early, 0), count),
            )
            lax.fori_loop(first, last, one, 0)
            return carry

        lax.fori_loop(0, groups, each, 0)

    def weigh(base, block):
        keys = rows_of(block)
        chains = [(h, base + a) for a in range(group) for h in range(heads)]
        lanes = [slice(h * head_size, (h + 1) * head_size) for h in range(heads)]
        held_state = [(peak[h, q], mass[h, q], blend[h, q]) for h, q in chains]
        asked = [q_ref[rows_of(q), lanes[h]] for h, q in chains]
        parts, soft, result = {}, {}, {}

        def score(i):
            h, q = chains[i]
            pieces = []
            for slot in range(frames):
                scores = lax.dot_general(
                    kv_ref[slot, 0, keys, lanes[h]], asked[i], (((1,), (1,)), ((), ())),
                    preferred_element_type=jnp.float32,
                )
                kept = mask_ref[h, q, sources[slot] + block] > 0
                pieces.append(scores * factor + jnp.where(kept, 0.0, NEGATIVE))
            parts[i] = pieces

        def soften(i):
            top, total, _ = held_state[i]
            new_top = top
            for p in parts[i]:
                new_top = jnp.maximum(new_top, jnp.max(p, axis=0, keepdims=True))
            fade = jnp.exp2(top - new_top)
            total = total * fade
            weights = [jnp.exp2(p - new_top) for p in parts[i]]
            for w in weights:
                total += jnp.sum(w, axis=0, keepdims=True)
            joined = jnp.concatenate([w.astype(jnp.bfloat16) for w in weights], axis=0)
            soft[i] = (new_top, total, fade, joined)

        def gather(i):
            h, q = chains[i]
            new_top, total, fade, joined = soft[i]
            values = jnp.concatenate(
                [kv_ref[slot, 1, keys, lanes[h]] for slot in range(frames)], axis=0
            )
            result[i] = new_top, total, held_state[i][2] * fade + lax.dot_general(
                values, joined, (((0,), (0,)), ((), ())), preferred_element_type=jnp.float32
            )

        for i in range(len(chains) + 2):
            if i < len(chains):
                score(i)
            if 0 <= i - 1 < len(chains):
                soften(i - 1)
            if 0 <= i - 2:
                gather(i - 2)
        for i, (h, q) in enumerate(chains):
            peak[h, q], mass[h, q], blend[h, q] = result[i]

    def settle(t):
        window = rows_of(t)
        for h in range(heads):
            lanes = slice(h * head_size, (h + 1) * head_size)
            done[me, window, lanes] = (blend[h, t] / mass[h, t]).T.astype(done.dtype)
        spread.own(t)

    peak[...] = jnp.full(peak.shape, NEGATIVE, jnp.float32)
    mass[...] = jnp.zeros(mass.shape, jnp.float32)
    blend[...] = jnp.zeros(blend.shape, jnp.float32)

    def turn(i, carry):
        @pl.when(jnp.logical_and(inside, i + AHEAD < count))
        def _():
            begin(i + AHEAD, 0)

        @pl.when(jnp.logical_and(inside, i == 1))
        def _():
            take()

        @pl.when(jnp.logical_and(inside, i == count + late))
        def _():
            share_out(1)

        relay.advance(i, count)

        @pl.when(i == count + late - 1)
        def _():
            give(True)

        @pl.when(i > late)
        def _():
            fold(i - late - 1)

        @pl.when(jnp.logical_and(i >= late, i < count + late))
        def _():
            step(i - late)

        @pl.when(jnp.logical_and(i > late, i < count + late - 1))
        def _():
            relay_pair(i - late - 1)

        return carry

    lax.fori_loop(0, count + late + 2, turn, 0)

    pass_band()

    def near(t, carry):
        spread.pass_all(t, False)
        return carry

    lax.fori_loop(jnp.where(inside, count - group, 0), count, near, 0)
    lay.wait()

    def out(t):
        spread.collect(t)
        window = rows_of(t)
        plane = full[...].reshape(heads_axis * inner, full.shape[2])
        total = contract([done[i, window, :] for i in range(heads_axis)], plane)
        if gate.shape[1] == cols:
            own = gate[...]
        else:
            own = gate[2:3, pl.ds(pl.multiple_of(me * cols, cols), cols)]
        wide_part = got[me, window, :].astype(jnp.float32)
        mixed[window, :] = (wide_part + own * total).astype(mixed.dtype)
        store(t).start()

    def store(t):
        window = rows_of(t)
        return pltpu.make_async_copy(
            mixed.at[window, :], out_ref.at[window, :], o_sem.at[0]
        )

    behind = line - 1

    def last(i, carry):
        spread.advance(i, count, True)

        @pl.when(i == behind)
        def _():
            band_rest(2 if square else frames - 1, 2).wait_recv()

        @pl.when(i >= behind)
        def _():
            out(i - behind)

        return carry

    lax.fori_loop(0, count + behind, last, 0)

    relay.drain()
    spread.drain()
    pltpu.make_async_copy(mixed, out_ref, o_sem.at[0]).wait()
    ref = kv_ref.at[pl.ds(0, frames - 1)]
    send(
        ref, ref, kv_send.at[0], kv_recv.at[0, 0], frame=target_of(frame, frames, 1)
    ).wait_send()
    bands().wait_send()
    band_rest(frames - 1, 2).wait_send()


def sublayer(frames, heads_axis, heads, tokens, modulation, weight, out_weight, mask, gate):
    rows, cols = tokens.shape
    inner = weight.shape[2]
    count = rows // BLK
    group = math.gcd(count, GROUP)
    line = heads_axis // 2
    away = pl.BlockSpec(memory_space=pl.ANY)
    held = pl.BlockSpec(memory_space=pltpu.HBM)
    sem = pltpu.SemaphoreType.DMA
    if cols % 128 == 0:
        def w_slice(ref, band, there):
            return ref.at[band, pl.ds(pl.multiple_of(there * cols, cols), cols)]
    else:
        out_weight = out_weight.reshape(inner, heads_axis, cols).transpose(1, 0, 2)

        def w_slice(ref, band, there):
            return ref.at[there, band, :]

    relay_sems = [sem((1,)), sem((line, count)), sem((1,)), sem((count,))]
    return pl.pallas_call(
        functools.partial(block_kernel, frames, heads_axis, heads, count, group, w_slice),
        in_specs=[
            held, held, held, held, held, held,
        ],
        out_specs=away,
        out_shape=jax.ShapeDtypeStruct((rows, cols), jnp.bfloat16),
        scratch_shapes=[
            pltpu.VMEM((heads_axis, rows, cols), jnp.bfloat16),
            pltpu.VMEM(weight.shape, jnp.bfloat16),
            pltpu.VMEM((rows, inner), jnp.bfloat16),
            pltpu.VMEM((frames, 2, rows, inner), jnp.bfloat16),
            pltpu.VMEM((heads_axis, inner // frames, cols), jnp.bfloat16),
            pltpu.VMEM((heads_axis, inner, cols), jnp.bfloat16),
            pltpu.VMEM((heads_axis, rows, inner), jnp.bfloat16),
            pltpu.VMEM((heads, count, 1, BLK), jnp.float32),
            pltpu.VMEM((heads, count, 1, BLK), jnp.float32),
            pltpu.VMEM((heads, count, inner // heads, BLK), jnp.float32),
            pltpu.VMEM((rows, cols), jnp.bfloat16),
            pltpu.VMEM(modulation.shape, jnp.float32),
            pltpu.VMEM(gate.shape, jnp.float32),
            pltpu.SMEM(mask.shape, jnp.int32),
            *relay_sems,
            *relay_sems,
            sem((1,)),
            sem((count, frames - 1)),
            sem((1,)),
            sem((1,)),
            sem((1,)),
            sem((3,)),
            sem((7,)),
            sem((1,)),
        ],
        compiler_params=pltpu.CompilerParams(
            collective_id=0, has_side_effects=True, vmem_limit_bytes=VMEM_BYTES
        ),
        name="sublayer",
    )(*[
        pltpu.with_memory_space_constraint(x, pltpu.HBM)
        for x in (tokens, modulation, weight, out_weight, mask, gate)
    ])


def shards(frames, heads_axis, tokens, qkv_weight, out_weight, modulation, block_mask):
    local_cols = tokens.shape[1]
    gate = modulation
    if local_cols % 128:
        head = lax.axis_index("head")
        gate = lax.dynamic_slice_in_dim(modulation[2:3], head * local_cols, local_cols, 1)
    return sublayer(
        frames, heads_axis, block_mask.shape[0], tokens, modulation, qkv_weight, out_weight,
        block_mask, gate,
    )


def solution(mesh):
    placed = (
        P("frame", "head"),
        P(None, None, "head"),
        P("head", None),
        P(),
        P("head", "frame", None),
    )
    body = functools.partial(shards, mesh.shape["frame"], mesh.shape["head"])
    return jax.shard_map(
        body, mesh=mesh, in_specs=placed, out_specs=P("frame", "head"), check_vma=False
    )
```

```python
import functools
import math

import jax
import jax.numpy as jnp
from jax import lax
from jax.experimental import pallas as pl
from jax.experimental.pallas import tpu as pltpu
from jax.sharding import PartitionSpec as P

BLK = 128
NEGATIVE = -1e30
EPSILON = 1e-06
LOG2E = math.log2(math.e)
FIRST = 2
AHEAD = 4
LAG = 2
GROUP = 4
VMEM_BYTES = 52 * 2**20


def source_of(me, size, step):
    if size & (size - 1) == 0:
        return lax.bitwise_xor(me, step)
    return lax.rem(me + size - step, size)


def target_of(me, size, step):
    if size & (size - 1) == 0:
        return lax.bitwise_xor(me, step)
    return lax.rem(me + step, size)


def chain(me, size):
    return me // 2, me % 2, me + 1 - 2 * (me % 2)


def send(src, dst, send_sem, recv_sem, **where):
    return pltpu.make_async_remote_copy(
        src_ref=src,
        dst_ref=dst,
        send_sem=send_sem,
        recv_sem=recv_sem,
        device_id=where,
        device_id_type=pl.DeviceIdType.MESH,
    )


class Relay:
    def __init__(self, me, size, buffer, span, sems):
        self.me, self.size, self.buffer, self.span = me, size, buffer, span
        self.spot, self.core, self.other = chain(me, size)
        self.line = size // 2
        self.far_send, self.far_recv, self.pair_send, self.pair_recv = sems

    def rows(self, block, chunk):
        start = pl.multiple_of(chunk * self.span, self.span)
        return self.buffer.at[block, pl.ds(start, self.span), :]

    def hop(self, block, chunk, away, source=None):
        ref = self.rows(block, chunk)
        return send(
            ref if source is None else source,
            ref,
            self.far_send.at[0],
            self.far_recv.at[block // 2, chunk],
            head=self.me + 2 * away,
        )

    def pair(self, block, chunk, source=None):
        ref = self.rows(block, chunk)
        return send(
            ref if source is None else source,
            ref,
            self.pair_send.at[0],
            self.pair_recv.at[chunk],
            head=self.other,
        )

    def own(self, chunk, source=None):
        for away in (1, -1):
            edge = self.spot < self.line - 1 if away > 0 else self.spot > 0

            @pl.when(edge)
            def _():
                self.hop(self.me, chunk, away, source).start()

        self.pair(self.me, chunk, source).start()

    def pass_on(self, chunk, distance, ends=None):
        for away in (1, -1):
            spot = self.spot - away * distance
            here = spot >= 0 if away > 0 else spot < self.line
            edge = self.spot < self.line - 1 if away > 0 else self.spot > 0
            block = spot * 2 + self.core
            if ends is not None:
                far = 0 if away > 0 else self.line - 1
                here = spot == far if ends else jnp.logical_and(here, spot != far)

            @pl.when(here)
            def _():
                self.hop(block, chunk, away).wait_recv()

                @pl.when(edge)
                def _():
                    self.hop(block, chunk, away).start()

                self.pair(block, chunk).start()

    def advance(self, turn, count, ends=None):
        for distance in range(1, self.line):
            chunk = turn - (distance - 1)

            @pl.when(jnp.logical_and(chunk >= 0, chunk < count))
            def _():
                self.pass_on(chunk, distance, ends)

    def pass_all(self, chunk, ends):
        for distance in range(1, self.line):
            self.pass_on(chunk, distance, ends)

    def collect(self, chunk):
        start = pl.multiple_of(chunk * self.span, self.span)
        ref = self.buffer.at[pl.ds(0, self.line), pl.ds(start, self.span), :]
        send(
            ref, ref, self.pair_send.at[0], self.pair_recv.at[chunk], head=self.other
        ).wait_recv()

    def sent(self, blocks, sem):
        ref = self.buffer.at[pl.ds(0, blocks)]
        send(ref, ref, sem, self.pair_recv.at[0], head=self.other).wait_send()

    def drain(self):
        self.sent(self.line, self.pair_send.at[0])
        for spot in range(self.line):
            up = spot + 1 if spot < self.line - 1 else 0
            down = self.line - spot if spot > 0 else 0
            if up + down:

                @pl.when(self.spot == spot)
                def _():
                    self.sent(up + down, self.far_send.at[0])


def greet(me, frame, heads_axis, frames):
    barrier = pltpu.get_barrier_semaphore()
    spot, _, other = chain(me, heads_axis)
    line = heads_axis // 2

    def hail(**where):
        pl.semaphore_signal(
            barrier, inc=1, device_id=where, device_id_type=pl.DeviceIdType.MESH
        )

    near = (1, 2) if frames == 4 else range(1, frames)
    for s in near:
        hail(frame=target_of(frame, frames, s))
    hail(head=other)

    @pl.when(spot > 0)
    def _():
        hail(head=me - 2)

    @pl.when(spot < line - 1)
    def _():
        hail(head=me + 2)

    below = jnp.where(spot > 0, 1, 0)
    above = jnp.where(spot < line - 1, 1, 0)
    pl.semaphore_wait(barrier, len(near) + 1 + below + above)


def roll_call(me, heads_axis, calls):
    spot, _, _ = chain(me, heads_axis)
    line = heads_axis // 2
    for way, from_edge, to_edge in ((1, spot > 0, spot < line - 1), (-1, spot < line - 1, spot > 0)):
        call = calls.at[0 if way > 0 else 1]

        @pl.when(from_edge)
        def _():
            pl.semaphore_wait(call, 1)

        @pl.when(to_edge)
        def _():
            pl.semaphore_signal(
                call, inc=1, device_id={"head": me + 2 * way},
                device_id_type=pl.DeviceIdType.MESH,
            )


def contract(parts, weight):
    cols = parts[0].shape[1]
    if cols % 128 == 0:
        return jnp.dot(
            jnp.concatenate(parts, axis=1), weight, preferred_element_type=jnp.float32
        )
    total = 0.0
    for i, part in enumerate(parts):
        total += jnp.dot(
            part, weight[i * cols : (i + 1) * cols], preferred_element_type=jnp.float32
        )
    return total


def block_kernel(
    frames, heads_axis, heads, count, group, w_slice, tokens, adjust, weight, out_weight, mask_in,
    gate_in, out_ref, got, held, q_ref, kv_ref, band_ref, full, done,
    peak, mass, blend, mixed, modulation, gate, mask_ref,
    t_far_send, t_far_recv, t_pair_send, t_pair_recv,
    h_far_send, h_far_recv, h_pair_send, h_pair_recv,
    kv_send, kv_recv, w_send, w_recv, x_send, x_recv, local, o_sem, calls,
):
    me, frame = lax.axis_index("head"), lax.axis_index("frame")
    rows, cols = tokens.shape
    span = rows // count
    inner = q_ref.shape[1]
    width = cols * heads_axis
    line = heads_axis // 2
    share = band_ref.shape[1]
    head_size = inner // heads
    factor = LOG2E / math.sqrt(head_size)
    inside = jnp.logical_and(me // 2 > 0, me // 2 < line - 1)

    load = pltpu.make_async_copy(weight, held, local.at[0])
    load.start()
    mine = pltpu.make_async_copy(tokens, got.at[me], local.at[1])
    mine.start()
    tune = pltpu.make_async_copy(adjust, modulation, local.at[4])
    tune.start()
    hide = pltpu.make_async_copy(mask_in, mask_ref, local.at[6])
    hide.start()
    open_gate = pltpu.make_async_copy(gate_in, gate, local.at[5])
    open_gate.start()
    band = pl.ds(pl.multiple_of(frame * share, share), share)
    keep = pltpu.make_async_copy(w_slice(out_weight, band, me), band_ref.at[me], local.at[2])
    keep.start()
    greet(me, frame, heads_axis, frames)
    relay = Relay(me, heads_axis, got, span, (t_far_send, t_far_recv, t_pair_send, t_pair_recv))
    spread = Relay(me, heads_axis, done, span, (h_far_send, h_far_recv, h_pair_send, h_pair_recv))

    def rows_of(chunk):
        return pl.ds(pl.multiple_of(chunk * span, span), span)

    def begin(chunk, carry):
        relay.own(chunk, tokens.at[rows_of(chunk), :])
        return carry

    square = frames == 4

    def to_frame(chunk, s):
        window = rows_of(chunk)
        return send(
            kv_ref.at[0, :, window, :],
            kv_ref.at[s, :, window, :],
            kv_send.at[0],
            kv_recv.at[chunk, s - 1],
            frame=target_of(frame, frames, s),
        )

    def over(chunk, half):
        window = rows_of(chunk)
        near, there = (1, 2) if half == 0 else (2, 1)
        return send(
            kv_ref.at[near, half, window, :],
            kv_ref.at[3, half, window, :],
            kv_send.at[0],
            kv_recv.at[chunk, 2],
            frame=target_of(frame, frames, there),
        )

    def far_pair(chunk):
        ref = kv_ref.at[3, :, rows_of(chunk), :]
        return send(
            ref, ref, kv_send.at[0], kv_recv.at[chunk, 2], frame=target_of(frame, frames, 1)
        )

    direct = (1, 2) if square else tuple(range(1, frames))

    def relay_pair(chunk):
        for half in range(2 if square else 0):
            to_frame(chunk, half + 1).wait_recv()
            over(chunk, half).start()

    def heard(chunk):
        if square:
            far_pair(chunk).wait_recv()
        else:
            for s in direct:
                to_frame(chunk, s).wait_recv()

    def to_head(s):
        there = target_of(me, heads_axis, s)
        return send(
            w_slice(out_weight, band, there), band_ref.at[me], w_send.at[0], w_recv.at[0],
            head=there,
        )

    def bands():
        ref = band_ref.at[pl.ds(0, heads_axis - 1)]
        return send(
            ref, ref, w_send.at[0], w_recv.at[0], head=target_of(me, heads_axis, 1)
        )

    lay = pltpu.make_async_copy(band_ref, full.at[:, band, :], local.at[3])

    part = heads_axis // 2

    def slot_of(s, p):
        return p if square and s == p + 1 else 2

    def band_to(s, p):
        some = pl.ds(p * part, part)
        return send(
            band_ref.at[some], full.at[some, band, :], x_send.at[0], x_recv.at[slot_of(s, p)],
            frame=target_of(frame, frames, s),
        )

    def band_over(p):
        near, there = (1, 2) if p == 0 else (2, 1)
        part_rows = pl.ds(pl.multiple_of(source_of(frame, frames, near) * share, share), share)
        ref = full.at[pl.ds(p * part, part), part_rows, :]
        return send(
            ref, ref, x_send.at[0], x_recv.at[2], frame=target_of(frame, frames, there)
        )

    def band_near(p):
        ref = full.at[pl.ds(p * part, part), pl.ds(0, share), :]
        return send(
            ref, ref, x_send.at[0], x_recv.at[p], frame=target_of(frame, frames, p + 1)
        )

    def band_rest(count_of, slot):
        ref = full.at[:, pl.ds(0, count_of * share), :]
        return send(
            ref, ref, x_send.at[0], x_recv.at[slot], frame=target_of(frame, frames, 1)
        )

    late = jnp.maximum(jnp.maximum(me // 2, line - 1 - me // 2) - 1, 0)

    def give(later):
        for s in range(1, heads_axis):
            spot = target_of(me, heads_axis, s) // 2
            edge = jnp.logical_or(spot == 0, spot == line - 1)
            wait = jnp.logical_and(edge, spot != me // 2)

            @pl.when(wait if later else jnp.logical_not(wait))
            def _():
                to_head(s).start()

    def share_out(turn):
        for s in direct:
            band_to(s, (turn + s + 1) % 2).start()

    def pass_band():
        for p in range(2 if square else 0):
            band_near(p).wait_recv()
            band_over(p).start()

    def take():
        keep.wait()
        bands().wait_recv()
        lay.start()
        share_out(0)

    lax.fori_loop(0, FIRST, begin, 0)
    roll_call(me, heads_axis, calls)
    give(False)
    lax.fori_loop(FIRST, jnp.where(inside, AHEAD, count), begin, 0)
    mine.wait()
    load.wait()
    tune.wait()
    hide.wait()
    open_gate.wait()

    def step(chunk):
        relay.collect(chunk)
        window = rows_of(chunk)
        total = jnp.zeros((span, cols), jnp.float32)
        for i in range(heads_axis):
            total += got[i, window, :].astype(jnp.float32)
        center = jnp.sum(total, axis=1, keepdims=True) / width
        square = jnp.zeros((span, cols), jnp.float32)
        for i in range(heads_axis):
            off = got[i, window, :].astype(jnp.float32) - center
            square += off * off
        inverse = lax.rsqrt(jnp.sum(square, axis=1, keepdims=True) / width + EPSILON)
        parts = []
        for i in range(heads_axis):
            wide_part = got[i, window, :].astype(jnp.float32)
            shift = modulation[0:1, i * cols : (i + 1) * cols]
            gain = modulation[1:2, i * cols : (i + 1) * cols]
            parts.append(
                ((wide_part - center) * inverse * (1.0 + gain) + shift).astype(jnp.bfloat16)
            )
        sums = [contract(parts, held[j]) for j in range(3)]
        q_ref[window, :] = sums[0].astype(q_ref.dtype)
        kv_ref[0, 0, window, :] = sums[1].astype(kv_ref.dtype)
        kv_ref[0, 1, window, :] = sums[2].astype(kv_ref.dtype)
        for s in direct:
            to_frame(chunk, s).start()

    sources = [source_of(frame, frames, s) * count for s in range(frames)]

    groups = count // group

    def fold(c):
        early = count - 1 - LAG
        key = jnp.where(c < count - 1, c - LAG, early)

        @pl.when(jnp.logical_and(key >= 0, c != count - 1))
        def _():
            heard(key)

        def each(g, carry):
            ready = (g + 1) * group - 1

            def one(k, carry):
                @pl.when(c == count - 1)
                def _():
                    for at, chunk in ((1, count - 2), (4, count - 1)):

                        @pl.when(k == min(at, early - 1))
                        def _():
                            relay_pair(chunk)

                    @pl.when(jnp.logical_and(k == early - 1, jnp.logical_not(inside)))
                    def _():
                        take()
                        share_out(1)

                @pl.when(jnp.logical_and(c == count, jnp.logical_and(g == 0, k > key)))
                def _():
                    heard(k)

                weigh(g * group, k)

                @pl.when(k == count - 1)
                def _():
                    for a in range(group):
                        settle(g * group + a)

                    @pl.when(jnp.logical_and(inside, g > 0))
                    def _():
                        for a in range(group):
                            spread.pass_all((g - 1) * group + a, False)

                return carry

            first = jnp.where(
                c < count - 1, jnp.where(c == ready, 0, jnp.maximum(key, 0)),
                jnp.where(c == count - 1, 0, key),
            )
            last = jnp.where(
                c < count - 1, jnp.where(c >= ready, key + 1, 0),
                jnp.where(c == count - 1, jnp.where(g == groups - 1, early, 0), count),
            )
            lax.fori_loop(first, last, one, 0)
            return carry

        lax.fori_loop(0, groups, each, 0)

    def weigh(base, block):
        keys = rows_of(block)
        chains = [(h, base + a) for a in range(group) for h in range(heads)]
        lanes = [slice(h * head_size, (h + 1) * head_size) for h in range(heads)]
        held_state = [(peak[h, q], mass[h, q], blend[h, q]) for h, q in chains]
        asked = [q_ref[rows_of(q), lanes[h]] for h, q in chains]
        parts, soft, result = {}, {}, {}

        def score(i):
            h, q = chains[i]
            pieces = []
            for slot in range(frames):
                scores = lax.dot_general(
                    kv_ref[slot, 0, keys, lanes[h]], asked[i], (((1,), (1,)), ((), ())),
                    preferred_element_type=jnp.float32,
                )
                kept = mask_ref[h, q, sources[slot] + block] > 0
                pieces.append(scores * factor + jnp.where(kept, 0.0, NEGATIVE))
            parts[i] = pieces

        def soften(i):
            top, total, _ = held_state[i]
            new_top = top
            for p in parts[i]:
                new_top = jnp.maximum(new_top, jnp.max(p, axis=0, keepdims=True))
            fade = jnp.exp2(top - new_top)
            total = total * fade
            weights = [jnp.exp2(p - new_top) for p in parts[i]]
            for w in weights:
                total += jnp.sum(w, axis=0, keepdims=True)
            joined = jnp.concatenate([w.astype(jnp.bfloat16) for w in weights], axis=0)
            soft[i] = (new_top, total, fade, joined)

        def gather(i):
            h, q = chains[i]
            new_top, total, fade, joined = soft[i]
            values = jnp.concatenate(
                [kv_ref[slot, 1, keys, lanes[h]] for slot in range(frames)], axis=0
            )
            result[i] = new_top, total, held_state[i][2] * fade + lax.dot_general(
                values, joined, (((0,), (0,)), ((), ())), preferred_element_type=jnp.float32
            )

        for i in range(len(chains) + 2):
            if i < len(chains):
                score(i)
            if 0 <= i - 1 < len(chains):
                soften(i - 1)
            if 0 <= i - 2:
                gather(i - 2)
        for i, (h, q) in enumerate(chains):
            peak[h, q], mass[h, q], blend[h, q] = result[i]

    def settle(t):
        window = rows_of(t)
        for h in range(heads):
            lanes = slice(h * head_size, (h + 1) * head_size)
            done[me, window, lanes] = (blend[h, t] / mass[h, t]).T.astype(done.dtype)
        spread.own(t)

    peak[...] = jnp.full(peak.shape, NEGATIVE, jnp.float32)
    mass[...] = jnp.zeros(mass.shape, jnp.float32)
    blend[...] = jnp.zeros(blend.shape, jnp.float32)

    def turn(i, carry):
        @pl.when(jnp.logical_and(inside, i + AHEAD < count))
        def _():
            begin(i + AHEAD, 0)

        @pl.when(jnp.logical_and(inside, i == 1))
        def _():
            take()

        @pl.when(jnp.logical_and(inside, i == count + late))
        def _():
            share_out(1)

        relay.advance(i, count)

        @pl.when(i == count + late - 1)
        def _():
            give(True)

        @pl.when(i > late)
        def _():
            fold(i - late - 1)

        @pl.when(jnp.logical_and(i >= late, i < count + late))
        def _():
            step(i - late)

        @pl.when(jnp.logical_and(i > late, i < count + late - 1))
        def _():
            relay_pair(i - late - 1)

        return carry

    lax.fori_loop(0, count + late + 2, turn, 0)

    pass_band()

    def near(t, carry):
        spread.pass_all(t, False)
        return carry

    lax.fori_loop(jnp.where(inside, count - group, 0), count, near, 0)
    lay.wait()

    both = math.gcd(count, 2)

    def tall(t):
        return pl.ds(pl.multiple_of(t * both * span, both * span), both * span)

    def out(t):
        for a in range(both):
            spread.collect(t * both + a)
        window = tall(t)
        plane = full[...].reshape(heads_axis * inner, full.shape[2])
        total = contract([done[i, window, :] for i in range(heads_axis)], plane)
        if gate.shape[1] == cols:
            own = gate[...]
        else:
            own = gate[2:3, pl.ds(pl.multiple_of(me * cols, cols), cols)]
        wide_part = got[me, window, :].astype(jnp.float32)
        mixed[window, :] = (wide_part + own * total).astype(mixed.dtype)
        pltpu.make_async_copy(mixed.at[window, :], out_ref.at[window, :], o_sem.at[0]).start()

    behind = line - 1

    def last(i, carry):
        spread.advance(i, count, True)

        @pl.when(i == behind + both - 1)
        def _():
            band_rest(2 if square else frames - 1, 2).wait_recv()

        @pl.when(jnp.logical_and(i >= behind, (i - behind) % both == both - 1))
        def _():
            out((i - behind) // both)

        return carry

    lax.fori_loop(0, count + behind, last, 0)

    relay.drain()
    spread.drain()
    pltpu.make_async_copy(mixed, out_ref, o_sem.at[0]).wait()
    ref = kv_ref.at[pl.ds(0, frames - 1)]
    send(
        ref, ref, kv_send.at[0], kv_recv.at[0, 0], frame=target_of(frame, frames, 1)
    ).wait_send()
    bands().wait_send()
    band_rest(frames - 1, 2).wait_send()


def sublayer(frames, heads_axis, heads, tokens, modulation, weight, out_weight, mask, gate):
    rows, cols = tokens.shape
    inner = weight.shape[2]
    count = rows // BLK
    group = math.gcd(count, GROUP)
    line = heads_axis // 2
    away = pl.BlockSpec(memory_space=pl.ANY)
    held = pl.BlockSpec(memory_space=pltpu.HBM)
    sem = pltpu.SemaphoreType.DMA
    if cols % 128 == 0:
        def w_slice(ref, band, there):
            return ref.at[band, pl.ds(pl.multiple_of(there * cols, cols), cols)]
    else:
        out_weight = out_weight.reshape(inner, heads_axis, cols).transpose(1, 0, 2)

        def w_slice(ref, band, there):
            return ref.at[there, band, :]

    relay_sems = [sem((1,)), sem((line, count)), sem((1,)), sem((count,))]
    return pl.pallas_call(
        functools.partial(block_kernel, frames, heads_axis, heads, count, group, w_slice),
        in_specs=[
            held, held, held, held, held, held,
        ],
        out_specs=away,
        out_shape=jax.ShapeDtypeStruct((rows, cols), jnp.bfloat16),
        scratch_shapes=[
            pltpu.VMEM((heads_axis, rows, cols), jnp.bfloat16),
            pltpu.VMEM(weight.shape, jnp.bfloat16),
            pltpu.VMEM((rows, inner), jnp.bfloat16),
            pltpu.VMEM((frames, 2, rows, inner), jnp.bfloat16),
            pltpu.VMEM((heads_axis, inner // frames, cols), jnp.bfloat16),
            pltpu.VMEM((heads_axis, inner, cols), jnp.bfloat16),
            pltpu.VMEM((heads_axis, rows, inner), jnp.bfloat16),
            pltpu.VMEM((heads, count, 1, BLK), jnp.float32),
            pltpu.VMEM((heads, count, 1, BLK), jnp.float32),
            pltpu.VMEM((heads, count, inner // heads, BLK), jnp.float32),
            pltpu.VMEM((rows, cols), jnp.bfloat16),
            pltpu.VMEM(modulation.shape, jnp.float32),
            pltpu.VMEM(gate.shape, jnp.float32),
            pltpu.SMEM(mask.shape, jnp.int32),
            *relay_sems,
            *relay_sems,
            sem((1,)),
            sem((count, frames - 1)),
            sem((1,)),
            sem((1,)),
            sem((1,)),
            sem((3,)),
            sem((7,)),
            sem((1,)),
            pltpu.SemaphoreType.REGULAR((2,)),
        ],
        compiler_params=pltpu.CompilerParams(
            collective_id=0, has_side_effects=True, vmem_limit_bytes=VMEM_BYTES
        ),
        name="sublayer",
    )(*[
        pltpu.with_memory_space_constraint(x, pltpu.HBM)
        for x in (tokens, modulation, weight, out_weight, mask, gate)
    ])


def shards(frames, heads_axis, tokens, qkv_weight, out_weight, modulation, block_mask):
    local_cols = tokens.shape[1]
    gate = modulation
    if local_cols % 128:
        head = lax.axis_index("head")
        gate = lax.dynamic_slice_in_dim(modulation[2:3], head * local_cols, local_cols, 1)
    return sublayer(
        frames, heads_axis, block_mask.shape[0], tokens, modulation, qkv_weight, out_weight,
        block_mask, gate,
    )


def solution(mesh):
    placed = (
        P("frame", "head"),
        P(None, None, "head"),
        P("head", None),
        P(),
        P("head", "frame", None),
    )
    body = functools.partial(shards, mesh.shape["frame"], mesh.shape["head"])
    return jax.shard_map(
        body, mesh=mesh, in_specs=placed, out_specs=P("frame", "head"), check_vma=False
    )
```

```python
import functools
import math

import jax
import jax.numpy as jnp
from jax import lax
from jax.experimental import pallas as pl
from jax.experimental.pallas import tpu as pltpu
from jax.sharding import PartitionSpec as P

BLK = 128
NEGATIVE = -1e30
EPSILON = 1e-06
LOG2E = math.log2(math.e)
FIRST = 2
OUTWARD = 6
INWARD = 2
LAG = 2
GROUP = 4
VMEM_BYTES = 52 * 2**20


def source_of(me, size, step):
    if size & (size - 1) == 0:
        return lax.bitwise_xor(me, step)
    return lax.rem(me + size - step, size)


def target_of(me, size, step):
    if size & (size - 1) == 0:
        return lax.bitwise_xor(me, step)
    return lax.rem(me + step, size)


def chain(me, size):
    return me // 2, me % 2, me + 1 - 2 * (me % 2)


def send(src, dst, send_sem, recv_sem, **where):
    return pltpu.make_async_remote_copy(
        src_ref=src,
        dst_ref=dst,
        send_sem=send_sem,
        recv_sem=recv_sem,
        device_id=where,
        device_id_type=pl.DeviceIdType.MESH,
    )


class Relay:
    def __init__(self, me, size, buffer, span, sems):
        self.me, self.size, self.buffer, self.span = me, size, buffer, span
        self.spot, self.core, self.other = chain(me, size)
        self.line = size // 2
        self.far_send, self.far_recv, self.pair_send, self.pair_recv = sems

    def rows(self, block, chunk):
        start = pl.multiple_of(chunk * self.span, self.span)
        return self.buffer.at[block, pl.ds(start, self.span), :]

    def hop(self, block, chunk, away, source=None):
        ref = self.rows(block, chunk)
        return send(
            ref if source is None else source,
            ref,
            self.far_send.at[0],
            self.far_recv.at[block // 2, chunk],
            head=self.me + 2 * away,
        )

    def pair(self, block, chunk, source=None):
        ref = self.rows(block, chunk)
        return send(
            ref if source is None else source,
            ref,
            self.pair_send.at[0],
            self.pair_recv.at[chunk],
            head=self.other,
        )

    def own(self, chunk, source=None, outward=None):
        low = self.spot < self.line // 2
        for away in (1, -1):
            edge = self.spot < self.line - 1 if away > 0 else self.spot > 0
            if outward is not None:
                edge = jnp.logical_and(edge, low == ((away < 0) == outward))

            @pl.when(edge)
            def _():
                self.hop(self.me, chunk, away, source).start()

        if outward is not False:
            self.pair(self.me, chunk, source).start()

    def pass_on(self, chunk, distance, ends=None):
        for away in (1, -1):
            spot = self.spot - away * distance
            here = spot >= 0 if away > 0 else spot < self.line
            edge = self.spot < self.line - 1 if away > 0 else self.spot > 0
            block = spot * 2 + self.core
            if ends is not None:
                far = 0 if away > 0 else self.line - 1
                here = spot == far if ends else jnp.logical_and(here, spot != far)

            @pl.when(here)
            def _():
                self.hop(block, chunk, away).wait_recv()

                @pl.when(edge)
                def _():
                    self.hop(block, chunk, away).start()

                self.pair(block, chunk).start()

    def advance(self, turn, count, ends=None):
        for distance in range(1, self.line):
            chunk = turn - (distance - 1)

            @pl.when(jnp.logical_and(chunk >= 0, chunk < count))
            def _():
                self.pass_on(chunk, distance, ends)

    def pass_all(self, chunk, ends):
        for distance in range(1, self.line):
            self.pass_on(chunk, distance, ends)

    def collect(self, chunk):
        start = pl.multiple_of(chunk * self.span, self.span)
        ref = self.buffer.at[pl.ds(0, self.line), pl.ds(start, self.span), :]
        send(
            ref, ref, self.pair_send.at[0], self.pair_recv.at[chunk], head=self.other
        ).wait_recv()

    def sent(self, blocks, sem):
        ref = self.buffer.at[pl.ds(0, blocks)]
        send(ref, ref, sem, self.pair_recv.at[0], head=self.other).wait_send()

    def drain(self):
        self.sent(self.line, self.pair_send.at[0])
        for spot in range(self.line):
            up = spot + 1 if spot < self.line - 1 else 0
            down = self.line - spot if spot > 0 else 0
            if up + down:

                @pl.when(self.spot == spot)
                def _():
                    self.sent(up + down, self.far_send.at[0])


def greet(me, frame, heads_axis, frames):
    barrier = pltpu.get_barrier_semaphore()
    spot, _, other = chain(me, heads_axis)
    line = heads_axis // 2

    def hail(**where):
        pl.semaphore_signal(
            barrier, inc=1, device_id=where, device_id_type=pl.DeviceIdType.MESH
        )

    near = (1, 2) if frames == 4 else range(1, frames)
    for s in near:
        hail(frame=target_of(frame, frames, s))
    hail(head=other)

    @pl.when(spot > 0)
    def _():
        hail(head=me - 2)

    @pl.when(spot < line - 1)
    def _():
        hail(head=me + 2)

    below = jnp.where(spot > 0, 1, 0)
    above = jnp.where(spot < line - 1, 1, 0)
    pl.semaphore_wait(barrier, len(near) + 1 + below + above)


def roll_call(me, heads_axis, calls):
    spot, _, _ = chain(me, heads_axis)
    line = heads_axis // 2
    for way, from_edge, to_edge in ((1, spot > 0, spot < line - 1), (-1, spot < line - 1, spot > 0)):
        call = calls.at[0 if way > 0 else 1]

        @pl.when(from_edge)
        def _():
            pl.semaphore_wait(call, 1)

        @pl.when(to_edge)
        def _():
            pl.semaphore_signal(
                call, inc=1, device_id={"head": me + 2 * way},
                device_id_type=pl.DeviceIdType.MESH,
            )


def contract(parts, weight):
    cols = parts[0].shape[1]
    if cols % 128 == 0:
        return jnp.dot(
            jnp.concatenate(parts, axis=1), weight, preferred_element_type=jnp.float32
        )
    total = 0.0
    for i, part in enumerate(parts):
        total += jnp.dot(
            part, weight[i * cols : (i + 1) * cols], preferred_element_type=jnp.float32
        )
    return total


def block_kernel(
    frames, heads_axis, heads, count, group, w_slice, tokens, adjust, weight, out_weight, mask_in,
    gate_in, out_ref, got, held, q_ref, kv_ref, band_ref, full, done,
    peak, mass, blend, mixed, modulation, gate, mask_ref,
    t_far_send, t_far_recv, t_pair_send, t_pair_recv,
    h_far_send, h_far_recv, h_pair_send, h_pair_recv,
    kv_send, kv_recv, w_send, w_recv, x_send, x_recv, local, o_sem, calls,
):
    me, frame = lax.axis_index("head"), lax.axis_index("frame")
    rows, cols = tokens.shape
    span = rows // count
    inner = q_ref.shape[1]
    width = cols * heads_axis
    line = heads_axis // 2
    share = band_ref.shape[1]
    head_size = inner // heads
    factor = LOG2E / math.sqrt(head_size)
    inside = jnp.logical_and(me // 2 > 0, me // 2 < line - 1)

    load = pltpu.make_async_copy(weight, held, local.at[0])
    load.start()
    mine = pltpu.make_async_copy(tokens, got.at[me], local.at[1])
    mine.start()
    tune = pltpu.make_async_copy(adjust, modulation, local.at[4])
    tune.start()
    hide = pltpu.make_async_copy(mask_in, mask_ref, local.at[6])
    hide.start()
    open_gate = pltpu.make_async_copy(gate_in, gate, local.at[5])
    open_gate.start()
    band = pl.ds(pl.multiple_of(frame * share, share), share)
    keep = pltpu.make_async_copy(w_slice(out_weight, band, me), band_ref.at[me], local.at[2])
    keep.start()
    greet(me, frame, heads_axis, frames)
    relay = Relay(me, heads_axis, got, span, (t_far_send, t_far_recv, t_pair_send, t_pair_recv))
    spread = Relay(me, heads_axis, done, span, (h_far_send, h_far_recv, h_pair_send, h_pair_recv))

    def rows_of(chunk):
        return pl.ds(pl.multiple_of(chunk * span, span), span)

    def begin(outward, chunk):
        relay.own(chunk, tokens.at[rows_of(chunk), :], outward)

    def launch(first, last, outward):
        def one(chunk, carry):
            begin(outward, chunk)
            return carry

        lax.fori_loop(first, last, one, 0)

    square = frames == 4

    def to_frame(chunk, s):
        window = rows_of(chunk)
        return send(
            kv_ref.at[0, :, window, :],
            kv_ref.at[s, :, window, :],
            kv_send.at[0],
            kv_recv.at[chunk, s - 1],
            frame=target_of(frame, frames, s),
        )

    def over(chunk, half):
        window = rows_of(chunk)
        near, there = (1, 2) if half == 0 else (2, 1)
        return send(
            kv_ref.at[near, half, window, :],
            kv_ref.at[3, half, window, :],
            kv_send.at[0],
            kv_recv.at[chunk, 2],
            frame=target_of(frame, frames, there),
        )

    def far_pair(chunk):
        ref = kv_ref.at[3, :, rows_of(chunk), :]
        return send(
            ref, ref, kv_send.at[0], kv_recv.at[chunk, 2], frame=target_of(frame, frames, 1)
        )

    direct = (1, 2) if square else tuple(range(1, frames))

    def relay_pair(chunk):
        for half in range(2 if square else 0):
            to_frame(chunk, half + 1).wait_recv()
            over(chunk, half).start()

    def heard(chunk):
        if square:
            far_pair(chunk).wait_recv()
        else:
            for s in direct:
                to_frame(chunk, s).wait_recv()

    def to_head(s):
        there = target_of(me, heads_axis, s)
        return send(
            w_slice(out_weight, band, there), band_ref.at[me], w_send.at[0], w_recv.at[0],
            head=there,
        )

    def bands():
        ref = band_ref.at[pl.ds(0, heads_axis - 1)]
        return send(
            ref, ref, w_send.at[0], w_recv.at[0], head=target_of(me, heads_axis, 1)
        )

    lay = pltpu.make_async_copy(band_ref, full.at[:, band, :], local.at[3])

    part = heads_axis // 2

    def slot_of(s, p):
        return p if square and s == p + 1 else 2

    def band_to(s, p):
        some = pl.ds(p * part, part)
        return send(
            band_ref.at[some], full.at[some, band, :], x_send.at[0], x_recv.at[slot_of(s, p)],
            frame=target_of(frame, frames, s),
        )

    def band_over(p):
        near, there = (1, 2) if p == 0 else (2, 1)
        part_rows = pl.ds(pl.multiple_of(source_of(frame, frames, near) * share, share), share)
        ref = full.at[pl.ds(p * part, part), part_rows, :]
        return send(
            ref, ref, x_send.at[0], x_recv.at[2], frame=target_of(frame, frames, there)
        )

    def band_near(p):
        ref = full.at[pl.ds(p * part, part), pl.ds(0, share), :]
        return send(
            ref, ref, x_send.at[0], x_recv.at[p], frame=target_of(frame, frames, p + 1)
        )

    def band_rest(count_of, slot):
        ref = full.at[:, pl.ds(0, count_of * share), :]
        return send(
            ref, ref, x_send.at[0], x_recv.at[slot], frame=target_of(frame, frames, 1)
        )

    late = jnp.maximum(jnp.maximum(me // 2, line - 1 - me // 2) - 1, 0)

    def give(later):
        for s in range(1, heads_axis):
            spot = target_of(me, heads_axis, s) // 2
            edge = jnp.logical_or(spot == 0, spot == line - 1)
            wait = jnp.logical_and(edge, spot != me // 2)

            @pl.when(wait if later else jnp.logical_not(wait))
            def _():
                to_head(s).start()

    def share_out(turn):
        for s in direct:
            band_to(s, (turn + s + 1) % 2).start()

    def pass_band():
        for p in range(2 if square else 0):
            band_near(p).wait_recv()
            band_over(p).start()

    def take():
        keep.wait()
        bands().wait_recv()
        lay.start()
        share_out(0)

    launch(0, FIRST, True)
    launch(0, FIRST, False)
    roll_call(me, heads_axis, calls)
    give(False)
    launch(FIRST, jnp.where(inside, OUTWARD, count), True)
    launch(FIRST, jnp.where(inside, INWARD, count), False)
    mine.wait()
    load.wait()
    tune.wait()
    hide.wait()
    open_gate.wait()

    def step(chunk):
        relay.collect(chunk)
        window = rows_of(chunk)
        total = jnp.zeros((span, cols), jnp.float32)
        for i in range(heads_axis):
            total += got[i, window, :].astype(jnp.float32)
        center = jnp.sum(total, axis=1, keepdims=True) / width
        square = jnp.zeros((span, cols), jnp.float32)
        for i in range(heads_axis):
            off = got[i, window, :].astype(jnp.float32) - center
            square += off * off
        inverse = lax.rsqrt(jnp.sum(square, axis=1, keepdims=True) / width + EPSILON)
        parts = []
        for i in range(heads_axis):
            wide_part = got[i, window, :].astype(jnp.float32)
            shift = modulation[0:1, i * cols : (i + 1) * cols]
            gain = modulation[1:2, i * cols : (i + 1) * cols]
            parts.append(
                ((wide_part - center) * inverse * (1.0 + gain) + shift).astype(jnp.bfloat16)
            )
        sums = [contract(parts, held[j]) for j in range(3)]
        q_ref[window, :] = sums[0].astype(q_ref.dtype)
        kv_ref[0, 0, window, :] = sums[1].astype(kv_ref.dtype)
        kv_ref[0, 1, window, :] = sums[2].astype(kv_ref.dtype)
        for s in direct:
            to_frame(chunk, s).start()

    sources = [source_of(frame, frames, s) * count for s in range(frames)]

    groups = count // group

    def fold(c):
        early = count - 1 - LAG
        key = jnp.where(c < count - 1, c - LAG, early)

        @pl.when(jnp.logical_and(key >= 0, c != count - 1))
        def _():
            heard(key)

        def each(g, carry):
            ready = (g + 1) * group - 1

            def one(k, carry):
                @pl.when(c == count - 1)
                def _():
                    for at, chunk in ((1, count - 2), (4, count - 1)):

                        @pl.when(k == min(at, early - 1))
                        def _():
                            relay_pair(chunk)

                    @pl.when(jnp.logical_and(k == early - 1, jnp.logical_not(inside)))
                    def _():
                        take()
                        share_out(1)

                @pl.when(jnp.logical_and(c == count, jnp.logical_and(g == 0, k > key)))
                def _():
                    heard(k)

                weigh(g * group, k)

                @pl.when(k == count - 1)
                def _():
                    for a in range(group):
                        settle(g * group + a)

                    @pl.when(jnp.logical_and(inside, g > 0))
                    def _():
                        for a in range(group):
                            spread.pass_all((g - 1) * group + a, False)

                return carry

            first = jnp.where(
                c < count - 1, jnp.where(c == ready, 0, jnp.maximum(key, 0)),
                jnp.where(c == count - 1, 0, key),
            )
            last = jnp.where(
                c < count - 1, jnp.where(c >= ready, key + 1, 0),
                jnp.where(c == count - 1, jnp.where(g == groups - 1, early, 0), count),
            )
            lax.fori_loop(first, last, one, 0)
            return carry

        lax.fori_loop(0, groups, each, 0)

    def weigh(base, block):
        keys = rows_of(block)
        chains = [(h, base + a) for a in range(group) for h in range(heads)]
        lanes = [slice(h * head_size, (h + 1) * head_size) for h in range(heads)]
        held_state = [(peak[h, q], mass[h, q], blend[h, q]) for h, q in chains]
        asked = [q_ref[rows_of(q), lanes[h]] for h, q in chains]
        parts, soft, result = {}, {}, {}

        def score(i):
            h, q = chains[i]
            pieces = []
            for slot in range(frames):
                scores = lax.dot_general(
                    kv_ref[slot, 0, keys, lanes[h]], asked[i], (((1,), (1,)), ((), ())),
                    preferred_element_type=jnp.float32,
                )
                kept = mask_ref[h, q, sources[slot] + block] > 0
                pieces.append(scores * factor + jnp.where(kept, 0.0, NEGATIVE))
            parts[i] = pieces

        def soften(i):
            top, total, _ = held_state[i]
            new_top = top
            for p in parts[i]:
                new_top = jnp.maximum(new_top, jnp.max(p, axis=0, keepdims=True))
            fade = jnp.exp2(top - new_top)
            total = total * fade
            weights = [jnp.exp2(p - new_top) for p in parts[i]]
            for w in weights:
                total += jnp.sum(w, axis=0, keepdims=True)
            joined = jnp.concatenate([w.astype(jnp.bfloat16) for w in weights], axis=0)
            soft[i] = (new_top, total, fade, joined)

        def gather(i):
            h, q = chains[i]
            new_top, total, fade, joined = soft[i]
            values = jnp.concatenate(
                [kv_ref[slot, 1, keys, lanes[h]] for slot in range(frames)], axis=0
            )
            result[i] = new_top, total, held_state[i][2] * fade + lax.dot_general(
                values, joined, (((0,), (0,)), ((), ())), preferred_element_type=jnp.float32
            )

        for i in range(len(chains) + 2):
            if i < len(chains):
                score(i)
            if 0 <= i - 1 < len(chains):
                soften(i - 1)
            if 0 <= i - 2:
                gather(i - 2)
        for i, (h, q) in enumerate(chains):
            peak[h, q], mass[h, q], blend[h, q] = result[i]

    def settle(t):
        window = rows_of(t)
        for h in range(heads):
            lanes = slice(h * head_size, (h + 1) * head_size)
            done[me, window, lanes] = (blend[h, t] / mass[h, t]).T.astype(done.dtype)
        spread.own(t)

    peak[...] = jnp.full(peak.shape, NEGATIVE, jnp.float32)
    mass[...] = jnp.zeros(mass.shape, jnp.float32)
    blend[...] = jnp.zeros(blend.shape, jnp.float32)

    def turn(i, carry):
        for outward, ahead in ((True, OUTWARD), (False, INWARD)):

            @pl.when(jnp.logical_and(inside, i + ahead < count))
            def _():
                begin(outward, i + ahead)

        @pl.when(jnp.logical_and(inside, i == 1))
        def _():
            take()

        @pl.when(jnp.logical_and(inside, i == count + late))
        def _():
            share_out(1)

        relay.advance(i, count)

        @pl.when(i == count + late - 1)
        def _():
            give(True)

        @pl.when(i > late)
        def _():
            fold(i - late - 1)

        @pl.when(jnp.logical_and(i >= late, i < count + late))
        def _():
            step(i - late)

        @pl.when(jnp.logical_and(i > late, i < count + late - 1))
        def _():
            relay_pair(i - late - 1)

        return carry

    lax.fori_loop(0, count + late + 2, turn, 0)

    pass_band()

    def near(t, carry):
        spread.pass_all(t, False)
        return carry

    lax.fori_loop(jnp.where(inside, count - group, 0), count, near, 0)
    lay.wait()

    both = math.gcd(count, 2)

    def tall(t):
        return pl.ds(pl.multiple_of(t * both * span, both * span), both * span)

    def out(t):
        for a in range(both):
            spread.collect(t * both + a)
        window = tall(t)
        plane = full[...].reshape(heads_axis * inner, full.shape[2])
        total = contract([done[i, window, :] for i in range(heads_axis)], plane)
        if gate.shape[1] == cols:
            own = gate[...]
        else:
            own = gate[2:3, pl.ds(pl.multiple_of(me * cols, cols), cols)]
        wide_part = got[me, window, :].astype(jnp.float32)
        mixed[window, :] = (wide_part + own * total).astype(mixed.dtype)
        pltpu.make_async_copy(mixed.at[window, :], out_ref.at[window, :], o_sem.at[0]).start()

    behind = line - 1

    def last(i, carry):
        spread.advance(i, count, True)

        @pl.when(i == behind + both - 1)
        def _():
            band_rest(2 if square else frames - 1, 2).wait_recv()

        @pl.when(jnp.logical_and(i >= behind, (i - behind) % both == both - 1))
        def _():
            out((i - behind) // both)

        return carry

    lax.fori_loop(0, count + behind, last, 0)

    relay.drain()
    spread.drain()
    pltpu.make_async_copy(mixed, out_ref, o_sem.at[0]).wait()
    ref = kv_ref.at[pl.ds(0, frames - 1)]
    send(
        ref, ref, kv_send.at[0], kv_recv.at[0, 0], frame=target_of(frame, frames, 1)
    ).wait_send()
    bands().wait_send()
    band_rest(frames - 1, 2).wait_send()


def sublayer(frames, heads_axis, heads, tokens, modulation, weight, out_weight, mask, gate):
    rows, cols = tokens.shape
    inner = weight.shape[2]
    count = rows // BLK
    group = math.gcd(count, GROUP)
    line = heads_axis // 2
    away = pl.BlockSpec(memory_space=pl.ANY)
    held = pl.BlockSpec(memory_space=pltpu.HBM)
    sem = pltpu.SemaphoreType.DMA
    if cols % 128 == 0:
        def w_slice(ref, band, there):
            return ref.at[band, pl.ds(pl.multiple_of(there * cols, cols), cols)]
    else:
        out_weight = out_weight.reshape(inner, heads_axis, cols).transpose(1, 0, 2)

        def w_slice(ref, band, there):
            return ref.at[there, band, :]

    relay_sems = [sem((1,)), sem((line, count)), sem((1,)), sem((count,))]
    return pl.pallas_call(
        functools.partial(block_kernel, frames, heads_axis, heads, count, group, w_slice),
        in_specs=[
            held, held, held, held, held, held,
        ],
        out_specs=away,
        out_shape=jax.ShapeDtypeStruct((rows, cols), jnp.bfloat16),
        scratch_shapes=[
            pltpu.VMEM((heads_axis, rows, cols), jnp.bfloat16),
            pltpu.VMEM(weight.shape, jnp.bfloat16),
            pltpu.VMEM((rows, inner), jnp.bfloat16),
            pltpu.VMEM((frames, 2, rows, inner), jnp.bfloat16),
            pltpu.VMEM((heads_axis, inner // frames, cols), jnp.bfloat16),
            pltpu.VMEM((heads_axis, inner, cols), jnp.bfloat16),
            pltpu.VMEM((heads_axis, rows, inner), jnp.bfloat16),
            pltpu.VMEM((heads, count, 1, BLK), jnp.float32),
            pltpu.VMEM((heads, count, 1, BLK), jnp.float32),
            pltpu.VMEM((heads, count, inner // heads, BLK), jnp.float32),
            pltpu.VMEM((rows, cols), jnp.bfloat16),
            pltpu.VMEM(modulation.shape, jnp.float32),
            pltpu.VMEM(gate.shape, jnp.float32),
            pltpu.SMEM(mask.shape, jnp.int32),
            *relay_sems,
            *relay_sems,
            sem((1,)),
            sem((count, frames - 1)),
            sem((1,)),
            sem((1,)),
            sem((1,)),
            sem((3,)),
            sem((7,)),
            sem((1,)),
            pltpu.SemaphoreType.REGULAR((2,)),
        ],
        compiler_params=pltpu.CompilerParams(
            collective_id=0, has_side_effects=True, vmem_limit_bytes=VMEM_BYTES
        ),
        name="sublayer",
    )(*[
        pltpu.with_memory_space_constraint(x, pltpu.HBM)
        for x in (tokens, modulation, weight, out_weight, mask, gate)
    ])


def shards(frames, heads_axis, tokens, qkv_weight, out_weight, modulation, block_mask):
    local_cols = tokens.shape[1]
    gate = modulation
    if local_cols % 128:
        head = lax.axis_index("head")
        gate = lax.dynamic_slice_in_dim(modulation[2:3], head * local_cols, local_cols, 1)
    return sublayer(
        frames, heads_axis, block_mask.shape[0], tokens, modulation, qkv_weight, out_weight,
        block_mask, gate,
    )


def solution(mesh):
    placed = (
        P("frame", "head"),
        P(None, None, "head"),
        P("head", None),
        P(),
        P("head", "frame", None),
    )
    body = functools.partial(shards, mesh.shape["frame"], mesh.shape["head"])
    return jax.shard_map(
        body, mesh=mesh, in_specs=placed, out_specs=P("frame", "head"), check_vma=False
    )
```

```python
import functools
import math

import jax
import jax.numpy as jnp
from jax import lax
from jax.experimental import pallas as pl
from jax.experimental.pallas import tpu as pltpu
from jax.sharding import PartitionSpec as P

BLK = 128
NEGATIVE = -1e30
EPSILON = 1e-06
LOG2E = math.log2(math.e)
FIRST = 2
OUTWARD = 6
INWARD = 2
LAG = 2
GROUP = 4
VMEM_BYTES = 52 * 2**20


def source_of(me, size, step):
    if size & (size - 1) == 0:
        return lax.bitwise_xor(me, step)
    return lax.rem(me + size - step, size)


def target_of(me, size, step):
    if size & (size - 1) == 0:
        return lax.bitwise_xor(me, step)
    return lax.rem(me + step, size)


def chain(me, size):
    return me // 2, me % 2, me + 1 - 2 * (me % 2)


def send(src, dst, send_sem, recv_sem, **where):
    return pltpu.make_async_remote_copy(
        src_ref=src,
        dst_ref=dst,
        send_sem=send_sem,
        recv_sem=recv_sem,
        device_id=where,
        device_id_type=pl.DeviceIdType.MESH,
    )


class Relay:
    def __init__(self, me, size, buffer, span, sems):
        self.me, self.size, self.buffer, self.span = me, size, buffer, span
        self.spot, self.core, self.other = chain(me, size)
        self.line = size // 2
        self.far_send, self.far_recv, self.pair_send, self.pair_recv = sems

    def rows(self, block, chunk):
        start = pl.multiple_of(chunk * self.span, self.span)
        return self.buffer.at[block, pl.ds(start, self.span), :]

    def hop(self, block, chunk, away, source=None):
        ref = self.rows(block, chunk)
        return send(
            ref if source is None else source,
            ref,
            self.far_send.at[0],
            self.far_recv.at[block // 2, chunk],
            head=self.me + 2 * away,
        )

    def pair(self, block, chunk, source=None):
        ref = self.rows(block, chunk)
        return send(
            ref if source is None else source,
            ref,
            self.pair_send.at[0],
            self.pair_recv.at[chunk],
            head=self.other,
        )

    def own(self, chunk, source=None, outward=None):
        low = self.spot < self.line // 2
        for away in (1, -1):
            edge = self.spot < self.line - 1 if away > 0 else self.spot > 0
            if outward is not None:
                edge = jnp.logical_and(edge, low == ((away < 0) == outward))

            @pl.when(edge)
            def _():
                self.hop(self.me, chunk, away, source).start()

        if outward is not False:
            self.pair(self.me, chunk, source).start()

    def pass_on(self, chunk, distance, ends=None):
        for away in (1, -1):
            spot = self.spot - away * distance
            here = spot >= 0 if away > 0 else spot < self.line
            edge = self.spot < self.line - 1 if away > 0 else self.spot > 0
            block = spot * 2 + self.core
            if ends is not None:
                far = 0 if away > 0 else self.line - 1
                here = spot == far if ends else jnp.logical_and(here, spot != far)

            @pl.when(here)
            def _():
                self.hop(block, chunk, away).wait_recv()

                @pl.when(edge)
                def _():
                    self.hop(block, chunk, away).start()

                self.pair(block, chunk).start()

    def advance(self, turn, count, ends=None):
        for distance in range(1, self.line):
            chunk = turn - (distance - 1)

            @pl.when(jnp.logical_and(chunk >= 0, chunk < count))
            def _():
                self.pass_on(chunk, distance, ends)

    def pass_all(self, chunk, ends):
        for distance in range(1, self.line):
            self.pass_on(chunk, distance, ends)

    def collect(self, chunk):
        start = pl.multiple_of(chunk * self.span, self.span)
        ref = self.buffer.at[pl.ds(0, self.line), pl.ds(start, self.span), :]
        send(
            ref, ref, self.pair_send.at[0], self.pair_recv.at[chunk], head=self.other
        ).wait_recv()

    def sent(self, blocks, sem):
        ref = self.buffer.at[pl.ds(0, blocks)]
        send(ref, ref, sem, self.pair_recv.at[0], head=self.other).wait_send()

    def drain(self):
        self.sent(self.line, self.pair_send.at[0])
        for spot in range(self.line):
            up = spot + 1 if spot < self.line - 1 else 0
            down = self.line - spot if spot > 0 else 0
            if up + down:

                @pl.when(self.spot == spot)
                def _():
                    self.sent(up + down, self.far_send.at[0])


def greet(me, frame, heads_axis, frames):
    barrier = pltpu.get_barrier_semaphore()
    spot, _, other = chain(me, heads_axis)
    line = heads_axis // 2

    def hail(**where):
        pl.semaphore_signal(
            barrier, inc=1, device_id=where, device_id_type=pl.DeviceIdType.MESH
        )

    near = (1, 2) if frames == 4 else range(1, frames)
    for s in near:
        hail(frame=target_of(frame, frames, s))
    hail(head=other)

    @pl.when(spot > 0)
    def _():
        hail(head=me - 2)

    @pl.when(spot < line - 1)
    def _():
        hail(head=me + 2)

    below = jnp.where(spot > 0, 1, 0)
    above = jnp.where(spot < line - 1, 1, 0)
    pl.semaphore_wait(barrier, len(near) + 1 + below + above)


def roll_call(me, heads_axis, calls):
    spot, _, _ = chain(me, heads_axis)
    line = heads_axis // 2
    for way, from_edge, to_edge in ((1, spot > 0, spot < line - 1), (-1, spot < line - 1, spot > 0)):
        call = calls.at[0 if way > 0 else 1]

        @pl.when(from_edge)
        def _():
            pl.semaphore_wait(call, 1)

        @pl.when(to_edge)
        def _():
            pl.semaphore_signal(
                call, inc=1, device_id={"head": me + 2 * way},
                device_id_type=pl.DeviceIdType.MESH,
            )


def contract(parts, weight):
    cols = parts[0].shape[1]
    if cols % 128 == 0:
        return jnp.dot(
            jnp.concatenate(parts, axis=1), weight, preferred_element_type=jnp.float32
        )
    total = 0.0
    for i, part in enumerate(parts):
        total += jnp.dot(
            part, weight[i * cols : (i + 1) * cols], preferred_element_type=jnp.float32
        )
    return total


def block_kernel(
    frames, heads_axis, heads, count, group, w_slice, tokens, adjust, weight, out_weight, mask_in,
    gate_in, out_ref, got, held, q_ref, kv_ref, band_ref, full, done,
    peak, mass, blend, mixed, modulation, gate, mask_ref,
    t_far_send, t_far_recv, t_pair_send, t_pair_recv,
    h_far_send, h_far_recv, h_pair_send, h_pair_recv,
    kv_send, kv_recv, w_send, w_recv, x_send, x_recv, local, o_sem, calls,
):
    me, frame = lax.axis_index("head"), lax.axis_index("frame")
    rows, cols = tokens.shape
    span = rows // count
    inner = q_ref.shape[1]
    width = cols * heads_axis
    line = heads_axis // 2
    share = band_ref.shape[1]
    head_size = inner // heads
    factor = LOG2E / math.sqrt(head_size)
    inside = jnp.logical_and(me // 2 > 0, me // 2 < line - 1)

    load = pltpu.make_async_copy(weight, held, local.at[0])
    load.start()
    mine = pltpu.make_async_copy(tokens, got.at[me], local.at[1])
    mine.start()
    tune = pltpu.make_async_copy(adjust, modulation, local.at[4])
    tune.start()
    hide = pltpu.make_async_copy(mask_in, mask_ref, local.at[6])
    hide.start()
    open_gate = pltpu.make_async_copy(gate_in, gate, local.at[5])
    open_gate.start()
    band = pl.ds(pl.multiple_of(frame * share, share), share)
    keep = pltpu.make_async_copy(w_slice(out_weight, band, me), band_ref.at[me], local.at[2])
    keep.start()
    greet(me, frame, heads_axis, frames)
    relay = Relay(me, heads_axis, got, span, (t_far_send, t_far_recv, t_pair_send, t_pair_recv))
    spread = Relay(me, heads_axis, done, span, (h_far_send, h_far_recv, h_pair_send, h_pair_recv))

    def rows_of(chunk):
        return pl.ds(pl.multiple_of(chunk * span, span), span)

    def begin(outward, chunk):
        relay.own(chunk, tokens.at[rows_of(chunk), :], outward)

    def launch(first, last, outward):
        def one(chunk, carry):
            begin(outward, chunk)
            return carry

        lax.fori_loop(first, last, one, 0)

    square = frames == 4

    def to_frame(chunk, s):
        window = rows_of(chunk)
        return send(
            kv_ref.at[0, :, window, :],
            kv_ref.at[s, :, window, :],
            kv_send.at[0],
            kv_recv.at[chunk, s - 1],
            frame=target_of(frame, frames, s),
        )

    def over(chunk, half):
        window = rows_of(chunk)
        near, there = (1, 2) if half == 0 else (2, 1)
        return send(
            kv_ref.at[near, half, window, :],
            kv_ref.at[3, half, window, :],
            kv_send.at[0],
            kv_recv.at[chunk, 2],
            frame=target_of(frame, frames, there),
        )

    def far_pair(chunk):
        ref = kv_ref.at[3, :, rows_of(chunk), :]
        return send(
            ref, ref, kv_send.at[0], kv_recv.at[chunk, 2], frame=target_of(frame, frames, 1)
        )

    direct = (1, 2) if square else tuple(range(1, frames))

    def relay_pair(chunk):
        for half in range(2 if square else 0):
            to_frame(chunk, half + 1).wait_recv()
            over(chunk, half).start()

    def heard(chunk):
        if square:
            far_pair(chunk).wait_recv()
        else:
            for s in direct:
                to_frame(chunk, s).wait_recv()

    def to_head(s):
        there = target_of(me, heads_axis, s)
        return send(
            w_slice(out_weight, band, there), band_ref.at[me], w_send.at[0], w_recv.at[0],
            head=there,
        )

    def bands():
        ref = band_ref.at[pl.ds(0, heads_axis - 1)]
        return send(
            ref, ref, w_send.at[0], w_recv.at[0], head=target_of(me, heads_axis, 1)
        )

    lay = pltpu.make_async_copy(band_ref, full.at[:, band, :], local.at[3])

    part = heads_axis // 2

    def slot_of(s, p):
        return p if square and s == p + 1 else 2

    def band_to(s, p):
        some = pl.ds(p * part, part)
        return send(
            band_ref.at[some], full.at[some, band, :], x_send.at[0], x_recv.at[slot_of(s, p)],
            frame=target_of(frame, frames, s),
        )

    def band_over(p):
        near, there = (1, 2) if p == 0 else (2, 1)
        part_rows = pl.ds(pl.multiple_of(source_of(frame, frames, near) * share, share), share)
        ref = full.at[pl.ds(p * part, part), part_rows, :]
        return send(
            ref, ref, x_send.at[0], x_recv.at[2], frame=target_of(frame, frames, there)
        )

    def band_near(p):
        ref = full.at[pl.ds(p * part, part), pl.ds(0, share), :]
        return send(
            ref, ref, x_send.at[0], x_recv.at[p], frame=target_of(frame, frames, p + 1)
        )

    def band_rest(count_of, slot):
        ref = full.at[:, pl.ds(0, count_of * share), :]
        return send(
            ref, ref, x_send.at[0], x_recv.at[slot], frame=target_of(frame, frames, 1)
        )

    late = jnp.maximum(jnp.maximum(me // 2, line - 1 - me // 2) - 1, 0)

    def give(later):
        for s in range(1, heads_axis):
            spot = target_of(me, heads_axis, s) // 2
            edge = jnp.logical_or(spot == 0, spot == line - 1)
            wait = jnp.logical_and(edge, spot != me // 2)

            @pl.when(wait if later else jnp.logical_not(wait))
            def _():
                to_head(s).start()

    def share_out(turn):
        for s in direct:
            band_to(s, (turn + s + 1) % 2).start()

    def pass_band():
        for p in range(2 if square else 0):
            band_near(p).wait_recv()
            band_over(p).start()

    def take():
        keep.wait()
        bands().wait_recv()
        lay.start()
        share_out(0)

    launch(0, FIRST, True)
    launch(0, FIRST, False)
    roll_call(me, heads_axis, calls)
    give(False)
    launch(FIRST, jnp.where(inside, OUTWARD, count), True)
    launch(FIRST, jnp.where(inside, INWARD, count), False)
    mine.wait()
    load.wait()
    tune.wait()
    hide.wait()
    open_gate.wait()

    def step(chunk):
        relay.collect(chunk)
        window = rows_of(chunk)
        total = jnp.zeros((span, cols), jnp.float32)
        for i in range(heads_axis):
            total += got[i, window, :].astype(jnp.float32)
        center = jnp.sum(total, axis=1, keepdims=True) / width
        square = jnp.zeros((span, cols), jnp.float32)
        for i in range(heads_axis):
            off = got[i, window, :].astype(jnp.float32) - center
            square += off * off
        inverse = lax.rsqrt(jnp.sum(square, axis=1, keepdims=True) / width + EPSILON)
        parts = []
        for i in range(heads_axis):
            wide_part = got[i, window, :].astype(jnp.float32)
            shift = modulation[0:1, i * cols : (i + 1) * cols]
            gain = modulation[1:2, i * cols : (i + 1) * cols]
            parts.append(
                ((wide_part - center) * inverse * (1.0 + gain) + shift).astype(jnp.bfloat16)
            )
        sums = [contract(parts, held[j]) for j in range(3)]
        q_ref[window, :] = sums[0].astype(q_ref.dtype)
        kv_ref[0, 0, window, :] = sums[1].astype(kv_ref.dtype)
        kv_ref[0, 1, window, :] = sums[2].astype(kv_ref.dtype)
        for s in direct:
            to_frame(chunk, s).start()

    sources = [source_of(frame, frames, s) * count for s in range(frames)]

    groups = count // group

    def fold(c):
        early = count - 1 - LAG
        key = jnp.where(c < count - 1, c - LAG, early)

        @pl.when(jnp.logical_and(key >= 0, c != count - 1))
        def _():
            heard(key)

        def each(g, carry):
            ready = (g + 1) * group - 1

            def one(k, carry):
                @pl.when(c == count - 1)
                def _():
                    for at, chunk in ((1, count - 2), (4, count - 1)):

                        @pl.when(k == min(at, early - 1))
                        def _():
                            relay_pair(chunk)

                    @pl.when(jnp.logical_and(k == early - 1, jnp.logical_not(inside)))
                    def _():
                        take()
                        share_out(1)

                @pl.when(jnp.logical_and(c == count, jnp.logical_and(g == 0, k > key)))
                def _():
                    heard(k)

                weigh(g * group, k)

                @pl.when(k == count - 1)
                def _():
                    for a in range(group):
                        settle(g * group + a)

                    @pl.when(jnp.logical_and(inside, g > 0))
                    def _():
                        for a in range(group):
                            spread.pass_all((g - 1) * group + a, False)

                return carry

            first = jnp.where(
                c < count - 1, jnp.where(c == ready, 0, jnp.maximum(key, 0)),
                jnp.where(c == count - 1, 0, key),
            )
            last = jnp.where(
                c < count - 1, jnp.where(c >= ready, key + 1, 0),
                jnp.where(c == count - 1, jnp.where(g == groups - 1, early, 0), count),
            )
            lax.fori_loop(first, last, one, 0)
            return carry

        lax.fori_loop(0, groups, each, 0)

    def weigh(base, block):
        keys = rows_of(block)
        chains = [(h, base + a) for a in range(group) for h in range(heads)]
        lanes = [slice(h * head_size, (h + 1) * head_size) for h in range(heads)]
        held_state = [(peak[h, q], mass[h, q], blend[h, q]) for h, q in chains]
        asked = [q_ref[rows_of(q), lanes[h]] for h, q in chains]
        parts, soft, result = {}, {}, {}

        def score(i):
            h, q = chains[i]
            pieces = []
            for slot in range(frames):
                scores = lax.dot_general(
                    kv_ref[slot, 0, keys, lanes[h]], asked[i], (((1,), (1,)), ((), ())),
                    preferred_element_type=jnp.float32,
                )
                kept = mask_ref[h, q, sources[slot] + block] > 0
                pieces.append(scores * factor + jnp.where(kept, 0.0, NEGATIVE))
            parts[i] = pieces

        def soften(i):
            top, total, _ = held_state[i]
            new_top = top
            for p in parts[i]:
                new_top = jnp.maximum(new_top, jnp.max(p, axis=0, keepdims=True))
            fade = jnp.exp2(top - new_top)
            total = total * fade
            weights = [jnp.exp2(p - new_top) for p in parts[i]]
            for w in weights:
                total += jnp.sum(w, axis=0, keepdims=True)
            joined = jnp.concatenate([w.astype(jnp.bfloat16) for w in weights], axis=0)
            soft[i] = (new_top, total, fade, joined)

        def gather(i):
            h, q = chains[i]
            new_top, total, fade, joined = soft[i]
            values = jnp.concatenate(
                [kv_ref[slot, 1, keys, lanes[h]] for slot in range(frames)], axis=0
            )
            result[i] = new_top, total, held_state[i][2] * fade + lax.dot_general(
                values, joined, (((0,), (0,)), ((), ())), preferred_element_type=jnp.float32
            )

        for i in range(len(chains) + 2):
            if i < len(chains):
                score(i)
            if 0 <= i - 1 < len(chains):
                soften(i - 1)
            if 0 <= i - 2:
                gather(i - 2)
        for i, (h, q) in enumerate(chains):
            peak[h, q], mass[h, q], blend[h, q] = result[i]

    def settle(t):
        window = rows_of(t)
        for h in range(heads):
            lanes = slice(h * head_size, (h + 1) * head_size)
            done[me, window, lanes] = (blend[h, t] / mass[h, t]).T.astype(done.dtype)
        spread.own(t)

    peak[...] = jnp.full(peak.shape, NEGATIVE, jnp.float32)
    mass[...] = jnp.zeros(mass.shape, jnp.float32)
    blend[...] = jnp.zeros(blend.shape, jnp.float32)

    def turn(i, carry):
        for outward, ahead in ((True, OUTWARD), (False, INWARD)):

            @pl.when(jnp.logical_and(inside, i + ahead < count))
            def _():
                begin(outward, i + ahead)

        @pl.when(jnp.logical_and(inside, i == 1))
        def _():
            take()

        @pl.when(jnp.logical_and(inside, i == count + late))
        def _():
            share_out(1)

        relay.advance(i, count)

        @pl.when(i == count + late - 1)
        def _():
            give(True)

        @pl.when(i > late)
        def _():
            fold(i - late - 1)

        @pl.when(jnp.logical_and(i >= late, i < count + late))
        def _():
            step(i - late)

        @pl.when(jnp.logical_and(i > late, i < count + late - 1))
        def _():
            relay_pair(i - late - 1)

        return carry

    lax.fori_loop(0, count + late + 2, turn, 0)

    pass_band()

    def near(t, carry):
        spread.pass_all(t, False)
        return carry

    lax.fori_loop(jnp.where(inside, count - group, 0), count, near, 0)
    lay.wait()

    both = 1

    def tall(t):
        return pl.ds(pl.multiple_of(t * both * span, both * span), both * span)

    def out(t):
        for a in range(both):
            spread.collect(t * both + a)
        window = tall(t)
        plane = full[...].reshape(heads_axis * inner, full.shape[2])
        total = contract([done[i, window, :] for i in range(heads_axis)], plane)
        if gate.shape[1] == cols:
            own = gate[...]
        else:
            own = gate[2:3, pl.ds(pl.multiple_of(me * cols, cols), cols)]
        wide_part = got[me, window, :].astype(jnp.float32)
        mixed[window, :] = (wide_part + own * total).astype(mixed.dtype)
        pltpu.make_async_copy(mixed.at[window, :], out_ref.at[window, :], o_sem.at[0]).start()

    behind = line - 1

    def last(i, carry):
        spread.advance(i, count, True)

        @pl.when(i == behind + both - 1)
        def _():
            band_rest(2 if square else frames - 1, 2).wait_recv()

        @pl.when(jnp.logical_and(i >= behind, (i - behind) % both == both - 1))
        def _():
            out((i - behind) // both)

        return carry

    lax.fori_loop(0, count + behind, last, 0)

    relay.drain()
    spread.drain()
    pltpu.make_async_copy(mixed, out_ref, o_sem.at[0]).wait()
    ref = kv_ref.at[pl.ds(0, frames - 1)]
    send(
        ref, ref, kv_send.at[0], kv_recv.at[0, 0], frame=target_of(frame, frames, 1)
    ).wait_send()
    bands().wait_send()
    band_rest(frames - 1, 2).wait_send()


def sublayer(frames, heads_axis, heads, tokens, modulation, weight, out_weight, mask, gate):
    rows, cols = tokens.shape
    inner = weight.shape[2]
    count = rows // BLK
    group = math.gcd(count, GROUP)
    line = heads_axis // 2
    away = pl.BlockSpec(memory_space=pl.ANY)
    held = pl.BlockSpec(memory_space=pltpu.HBM)
    sem = pltpu.SemaphoreType.DMA
    if cols % 128 == 0:
        def w_slice(ref, band, there):
            return ref.at[band, pl.ds(pl.multiple_of(there * cols, cols), cols)]
    else:
        out_weight = out_weight.reshape(inner, heads_axis, cols).transpose(1, 0, 2)

        def w_slice(ref, band, there):
            return ref.at[there, band, :]

    relay_sems = [sem((1,)), sem((line, count)), sem((1,)), sem((count,))]
    return pl.pallas_call(
        functools.partial(block_kernel, frames, heads_axis, heads, count, group, w_slice),
        in_specs=[
            held, held, held, held, held, held,
        ],
        out_specs=away,
        out_shape=jax.ShapeDtypeStruct((rows, cols), jnp.bfloat16),
        scratch_shapes=[
            pltpu.VMEM((heads_axis, rows, cols), jnp.bfloat16),
            pltpu.VMEM(weight.shape, jnp.bfloat16),
            pltpu.VMEM((rows, inner), jnp.bfloat16),
            pltpu.VMEM((frames, 2, rows, inner), jnp.bfloat16),
            pltpu.VMEM((heads_axis, inner // frames, cols), jnp.bfloat16),
            pltpu.VMEM((heads_axis, inner, cols), jnp.bfloat16),
            pltpu.VMEM((heads_axis, rows, inner), jnp.bfloat16),
            pltpu.VMEM((heads, count, 1, BLK), jnp.float32),
            pltpu.VMEM((heads, count, 1, BLK), jnp.float32),
            pltpu.VMEM((heads, count, inner // heads, BLK), jnp.float32),
            pltpu.VMEM((rows, cols), jnp.bfloat16),
            pltpu.VMEM(modulation.shape, jnp.float32),
            pltpu.VMEM(gate.shape, jnp.float32),
            pltpu.SMEM(mask.shape, jnp.int32),
            *relay_sems,
            *relay_sems,
            sem((1,)),
            sem((count, frames - 1)),
            sem((1,)),
            sem((1,)),
            sem((1,)),
            sem((3,)),
            sem((7,)),
            sem((1,)),
            pltpu.SemaphoreType.REGULAR((2,)),
        ],
        compiler_params=pltpu.CompilerParams(
            collective_id=0, has_side_effects=True, vmem_limit_bytes=VMEM_BYTES
        ),
        name="sublayer",
    )(*[
        pltpu.with_memory_space_constraint(x, pltpu.HBM)
        for x in (tokens, modulation, weight, out_weight, mask, gate)
    ])


def shards(frames, heads_axis, tokens, qkv_weight, out_weight, modulation, block_mask):
    local_cols = tokens.shape[1]
    gate = modulation
    if local_cols % 128:
        head = lax.axis_index("head")
        gate = lax.dynamic_slice_in_dim(modulation[2:3], head * local_cols, local_cols, 1)
    return sublayer(
        frames, heads_axis, block_mask.shape[0], tokens, modulation, qkv_weight, out_weight,
        block_mask, gate,
    )


def solution(mesh):
    placed = (
        P("frame", "head"),
        P(None, None, "head"),
        P("head", None),
        P(),
        P("head", "frame", None),
    )
    body = functools.partial(shards, mesh.shape["frame"], mesh.shape["head"])
    return jax.shard_map(
        body, mesh=mesh, in_specs=placed, out_specs=P("frame", "head"), check_vma=False
    )
```
